32 devices in a mesh: row: 2 (over y), col: 16 (over z, x, core).
Axes of the slice: x: 2, y: 2, z: 4, core: 2. Of those that a mesh axis runs over, the one named last changes fastest.
Arguments:
- object_field: float32 [2, 2, 768, 6144], P(None, None, 'row', 'col'), may hold values from -5 to 5
- offsets: int32 [8, 16, 2], P('row', 'col'), may hold values from 0 to 256
- amplitudes: float32 [8, 16, 256, 256], P('row', 'col'), may hold values from 0.3 to 3
- probe: float32 [2, 256, 256], replicated, may hold values from -5 to 5
- phase: float32 [256, 256], replicated, may hold values from -3.140625 to 3.140625
Outputs:
- object_grad: float32 [2, 2, 768, 6144], P(None, None, 'row', 'col')
- probe_grad: float32 [2, 256, 256], replicated
The draws below stay inside these ranges and needn't reach their ends.
All inputs are finite; a program needn't handle non-finite values.
Results may differ from the reference program's by a relative error of at most 0.0003.
Values sent between devices are 32-bit elements; how exact they have to be, the bound alone decides.
No kernel may reach another device: no remote copies, remote signals or barrier semaphores. Data moves between devices by JAX's collectives and lax.ppermute only.
A program may use at most 64 MiB of HBM per device.

```python
import math
import jax
import jax.numpy as jnp
from jax import lax

SLICES = 2
TILE = 384
HALO = 64
PROBE = 256
POS = 4
NX = 768
NY = 6144
NROWPOS = 8
POSITIONS = 128
N_COL = 16


def set_ends(values, own_key, least, top_value):
    place = [jax.random.randint(jax.random.fold_in(own_key, axis), (), 0, length) for axis, length in enumerate(values.shape)]
    widest = values.shape.index(max(values.shape))
    next_to = place[:widest] + [(place[widest] + 1) % values.shape[widest]] + place[widest + 1:]
    return values.at[tuple(place)].set(least).at[tuple(next_to)].set(top_value)


def levels(stream_key, shape, pieces, least, top_value):
    def one(dim, parts):
        heights = jax.random.uniform(jax.random.fold_in(jax.random.fold_in(stream_key, 6), dim), (parts,), jnp.float32, least / len(pieces), top_value / len(pieces))
        return jnp.repeat(jnp.exp(heights), shape[dim] // parts).reshape((-1,) + (1,) * (len(shape) - dim - 1))

    gain = one(*pieces[0])
    for cut in pieces[1:]:
        gain = gain * one(*cut)
    return gain


def gaussian(stream_key, extent, scale, bound, split=(), held_as=jnp.bfloat16):
    drawn = scale * jax.random.normal(stream_key, extent, jnp.float32)
    if split:
        drawn = drawn * levels(stream_key, extent, split, -0.22, 0.18)
    return jnp.clip(drawn, -bound, bound).astype(held_as)


def setup_inputs(seed: int = 0) -> dict:
    seeds = jax.random.split(jax.random.key(seed), 6)
    return {
        "object_field": gaussian(seeds[0], (SLICES, 2, NX, NY), 0.7, 5.0, ((2, 2), (3, 16)), jnp.float32),
        "offsets": set_ends(jax.random.randint(seeds[1], (NROWPOS, N_COL, 2), 0, TILE + 2 * HALO - PROBE + 1), jax.random.fold_in(seeds[1], 1), 0, TILE + 2 * HALO - PROBE).astype(jnp.int32),
        "amplitudes": jnp.clip(jnp.exp(math.log(3.0) - 2.3025851 * jax.random.uniform(seeds[2], (NROWPOS, N_COL, PROBE, PROBE), jnp.float32) ** levels(seeds[2], (NROWPOS, N_COL, PROBE, PROBE), ((0, 2), (1, 16)), -0.2, 0.2)), 0.3, 3.0),
        "probe": gaussian(seeds[3], (2, PROBE, PROBE), 0.7, 5.0, (), jnp.float32),
        "phase": jnp.clip(jax.random.uniform(seeds[4], (PROBE, PROBE), jnp.float32, -3.140625, 3.140625), -3.140625, 3.140625),
    }


def reference(object_field, offsets, amplitudes, probe, phase):
    obj = lax.complex(object_field[:, 0], object_field[:, 1])
    padded = jnp.pad(obj, ((0, 0), (HALO, HALO), (HALO, HALO)), mode='wrap')
    probe_c = lax.complex(probe[0], probe[1])
    prop = lax.complex(jnp.cos(phase), jnp.sin(phase))
    flat_off = offsets.reshape(NROWPOS * N_COL, 2)
    flat_amp = amplitudes.reshape(NROWPOS * N_COL, PROBE, PROBE)
    accum = jnp.zeros(padded.shape, padded.dtype)
    probe_acc = jnp.zeros(probe_c.shape, probe_c.dtype)

    def fwd(x):
        return jnp.fft.fft2(x, norm='ortho')

    def inv(x):
        return jnp.fft.ifft2(x, norm='ortho')

    def one_step(carry, index):
        accum, probe_acc = carry
        row_dev = index // N_COL // POS
        col_dev = index % N_COL
        start_r = (row_dev * TILE + flat_off[index, 0]).astype(jnp.int32)
        start_c = (col_dev * TILE + flat_off[index, 1]).astype(jnp.int32)
        zero = jnp.zeros((), jnp.int32)
        wins = lax.dynamic_slice(padded, (zero, start_r, start_c), (SLICES, PROBE, PROBE))
        psis = []
        psi = probe_c
        exit_wave = None
        for s in range(SLICES):
            psis.append(psi)
            exit_wave = psi * wins[s]
            if s < SLICES - 1:
                psi = inv(prop * fwd(exit_wave))
        far = fwd(exit_wave)
        magnitude = jnp.sqrt(jnp.real(far) ** 2 + jnp.imag(far) ** 2)
        chi = far - flat_amp[index] * far / jnp.maximum(magnitude, 0.5)
        back = inv(chi)
        grads = [None] * SLICES
        for s in range(SLICES - 1, -1, -1):
            grads[s] = jnp.conj(psis[s]) * back
            if s > 0:
                back = inv(jnp.conj(prop) * fwd(jnp.conj(wins[s]) * back))
            else:
                probe_acc = probe_acc + jnp.conj(wins[0]) * back
        current = lax.dynamic_slice(accum, (zero, start_r, start_c), (SLICES, PROBE, PROBE))
        accum = lax.dynamic_update_slice(accum, current + jnp.stack(grads), (zero, start_r, start_c))
        return ((accum, probe_acc), None)
    (accum, probe_acc), _ = lax.scan(one_step, (accum, probe_acc), jnp.arange(NROWPOS * N_COL, dtype=jnp.int32))
    accum = accum.at[:, NX:NX + HALO, :].add(accum[:, 0:HALO, :])
    accum = accum.at[:, HALO:2 * HALO, :].add(accum[:, NX + HALO:NX + 2 * HALO, :])
    accum = accum[:, HALO:NX + HALO, :]
    accum = accum.at[:, :, NY:NY + HALO].add(accum[:, :, 0:HALO])
    accum = accum.at[:, :, HALO:2 * HALO].add(accum[:, :, NY + HALO:NY + 2 * HALO])
    accum = accum[:, :, HALO:NY + HALO]
    object_grad = jnp.stack([jnp.real(accum), jnp.imag(accum)], axis=1)
    scale = 1.0 / jnp.sqrt(jnp.asarray(POSITIONS, jnp.real(probe_acc).dtype))
    probe_grad = jnp.stack([jnp.real(probe_acc), jnp.imag(probe_acc)]) * scale
    return (object_grad, probe_grad)
```

```python
import functools
import math

import jax
import jax.numpy as jnp
import numpy as np
from jax import lax
from jax.experimental import pallas as pl
from jax.experimental.pallas import tpu as pltpu
from jax.sharding import PartitionSpec as P

HALO = 64
LANES = 128
F32 = jnp.float32
BF16 = jnp.bfloat16
VMEM = pl.BlockSpec(memory_space=pltpu.VMEM)
SMEM = pl.BlockSpec(memory_space=pltpu.SMEM)


def tables(size):
    half = size // 2
    n = np.arange(half)[:, None]
    k = np.arange(half)[None, :]
    parts = []
    for frequency in (2 * k, 2 * k + 1):
        angle = -2.0 * math.pi * (n * frequency % size) / size
        re, im = np.cos(angle) / math.sqrt(size), np.sin(angle) / math.sqrt(size)
        block = np.block([[re, im], [-im, re]]).astype(np.float32)
        for matrix in (block, block.T):
            high = matrix.astype(jnp.bfloat16)
            low = (matrix - high.astype(np.float32)).astype(jnp.bfloat16)
            parts += [high, low]
    return np.stack(parts)


def split(x):
    high = x.astype(BF16)
    return high, (x - high.astype(F32)).astype(BF16)


def dot(a, b):
    return jnp.dot(a, b, preferred_element_type=F32)


def right(x, t_ref, which):
    high, low = split(x)
    th, tl = t_ref[2 * which], t_ref[2 * which + 1]
    return dot(high, th) + dot(low, th) + dot(high, tl)


def left(t_ref, which, x):
    high, low = split(x)
    th, tl = t_ref[2 * which], t_ref[2 * which + 1]
    return dot(th, high) + dot(th, low) + dot(tl, high)


def forward(t_ref, xr, xi):
    h = xr.shape[0] // 2
    even = right(jnp.concatenate([xr[:, :h] + xr[:, h:], xi[:, :h] + xi[:, h:]], 1), t_ref, 0)
    odd = right(jnp.concatenate([xr[:, :h] - xr[:, h:], xi[:, :h] - xi[:, h:]], 1), t_ref, 2)
    yr = jnp.concatenate([even[:, :h], odd[:, :h]], 1)
    yi = jnp.concatenate([even[:, h:], odd[:, h:]], 1)
    even = left(t_ref, 1, jnp.concatenate([yr[:h] + yr[h:], yi[:h] + yi[h:]], 0))
    odd = left(t_ref, 3, jnp.concatenate([yr[:h] - yr[h:], yi[:h] - yi[h:]], 0))
    zr = jnp.concatenate([even[:h], odd[:h]], 0)
    zi = jnp.concatenate([even[h:], odd[h:]], 0)
    return zr, zi


def inverse(t_ref, zr, zi):
    h = zr.shape[0] // 2
    even = left(t_ref, 0, jnp.concatenate([zr[:h], zi[:h]], 0))
    odd = left(t_ref, 2, jnp.concatenate([zr[h:], zi[h:]], 0))
    p, m = even + odd, even - odd
    yr = jnp.concatenate([p[:h], m[:h]], 0)
    yi = jnp.concatenate([p[h:], m[h:]], 0)
    even = right(jnp.concatenate([yr[:, :h], yi[:, :h]], 1), t_ref, 1)
    odd = right(jnp.concatenate([yr[:, h:], yi[:, h:]], 1), t_ref, 3)
    p, m = even + odd, even - odd
    return jnp.concatenate([p[:, :h], m[:, :h]], 1), jnp.concatenate([p[:, h:], m[:, h:]], 1)


def call(kernel, out_shape, flops=0, **kwargs):
    return pl.pallas_call(
        kernel,
        out_shape=out_shape,
        cost_estimate=pl.CostEstimate(flops=flops, bytes_accessed=4 << 20, transcendentals=0),
        compiler_params=pltpu.CompilerParams(vmem_limit_bytes=56 << 20),
        **kwargs,
    )


def shaped(*shape):
    return jax.ShapeDtypeStruct(shape, F32)


def side_by_side(re, im):
    lane = lax.broadcasted_iota(jnp.int32, re.shape, 1)
    turned = pltpu.roll(im, HALO, 1)
    return lane < HALO, turned


def high_rim(re, im):
    low, turned = side_by_side(re, im)
    return jnp.where(low, turned, re)


def low_rim(re, im):
    low, turned = side_by_side(re, im)
    return jnp.where(low, re, turned)


def rims_kernel(x_ref, high_ref, low_ref):
    for s in range(x_ref.shape[0]):
        high_ref[s] = high_rim(x_ref[s, 0, :, -LANES:], x_ref[s, 1, :, -LANES:])
        low_ref[s] = low_rim(x_ref[s, 0, :, :LANES], x_ref[s, 1, :, :LANES])


def rims(x):
    slices, _, rows, _ = x.shape
    out = shaped(slices, rows, LANES)
    return call(rims_kernel, (out, out), in_specs=[VMEM], out_specs=(VMEM, VMEM))(x)


def exact(x):
    first = x.astype(BF16)
    rest = x - first.astype(F32)
    second = rest.astype(BF16)
    return first, second, (rest - second.astype(F32)).astype(BF16)


def unmixed(x):
    size = x.shape[1]
    half = size // 2

    def choose(dim):
        i = lax.broadcasted_iota(jnp.int32, (size, size), dim)
        j = lax.broadcasted_iota(jnp.int32, (size, size), 1 - dim)
        picked = jnp.where(j < half, 2 * j, 2 * (j - half) + 1)
        return jnp.where(i == picked, 1.0, 0.0).astype(BF16)

    across, down = choose(0), choose(1)
    a, b, c = exact(x)
    a, b, c = exact(dot(a, across) + dot(b, across) + dot(c, across))
    return dot(down, a) + dot(down, b) + dot(down, c)


def prepare_kernel(phase_ref, amp_ref, prop_ref, out_ref):
    phase = unmixed(phase_ref[...])
    prop_ref[0] = jnp.cos(phase)
    prop_ref[1] = jnp.sin(phase)

    @pl.loop(0, amp_ref.shape[0])
    def _(p):
        out_ref[p] = unmixed(amp_ref[p])


def prepare(phase, amplitudes):
    count, size, _ = amplitudes.shape
    return call(
        prepare_kernel,
        (shaped(2, size, size), shaped(count, size, size)),
        flops=1 << 29,
        in_specs=[VMEM, VMEM],
        out_specs=(VMEM, VMEM),
    )(phase, amplitudes)


def assemble(ext, tile, rows, high, low, corner_high, corner_low):
    size = tile.shape[1]
    end = LANES + size
    spans = ((0, rows, 0, HALO), (HALO, None, 0, size), (HALO + size, rows, HALO, HALO))
    for top, strip, source, length in spans:
        here = pl.ds(top, length)
        there = pl.ds(source, length)
        for c in range(2):
            ext[c, here, LANES:end] = tile[c] if strip is None else strip[c, there, :]
        h = high[...] if strip is None else corner_high[there, :]
        w = low[...] if strip is None else corner_low[there, :]
        ext[0, here, 0:LANES] = h
        ext[1, here, 0:LANES] = pltpu.roll(h, HALO, 1)
        ext[0, here, end : end + LANES] = w
        ext[1, here, end : end + LANES] = pltpu.roll(w, HALO, 1)


def place(off_ref, p):
    row = off_ref[p, 0]
    col = off_ref[p, 1] + HALO
    base = pl.multiple_of(col // LANES * LANES, LANES)
    return row // 8 * 8, row % 8, base, col % LANES


def window(ext, off_ref, p, c, size):
    row, dr, base, dc = place(off_ref, p)
    slab = ext[c, pl.ds(pl.multiple_of(row, 8), size + 8), pl.ds(base, size + LANES)]
    wide, tall = size + LANES, size + 8
    slab = pltpu.roll(slab, wide - dc, 1)[:, :size]
    return pltpu.roll(slab, tall - dr, 0)[:size]


def add_window(acc, off_ref, p, c, value):
    size = value.shape[0]
    row, dr, base, dc = place(off_ref, p)
    value = jnp.concatenate([value, jnp.zeros((8, size), F32)], 0)
    value = pltpu.roll(value, dr, 0)
    value = jnp.concatenate([value, jnp.zeros((size + 8, LANES), F32)], 1)
    value = pltpu.roll(value, dc, 1)
    at = (c, pl.ds(pl.multiple_of(row, 8), size + 8), pl.ds(base, size + LANES))
    acc[at] = acc[at] + value


def times(ar, ai, br, bi):
    return ar * br - ai * bi, ar * bi + ai * br


def conj_times(ar, ai, br, bi):
    return ar * br + ai * bi, ar * bi - ai * br


def first_kernel(off, tile, rows, high, low, ch, cl, probe, prop, t, psi_out, w_out, ext):
    p = pl.program_id(0)
    size = probe.shape[1]

    @pl.when(p == 0)
    def _():
        assemble(ext, tile, rows, high, low, ch, cl)

    wr, wi = window(ext, off, p, 0, size), window(ext, off, p, 1, size)
    w_out[0, 0] = wr
    w_out[0, 1] = wi
    fr, fi = forward(t, *times(probe[0], probe[1], wr, wi))
    xr, xi = inverse(t, *times(prop[0], prop[1], fr, fi))
    psi_out[0, 0] = xr
    psi_out[0, 1] = xi


def leave(acc, tile_out, high_out, low_out, span):
    end = acc.shape[2] - LANES
    for c in range(2):
        tile_out[c] = acc[c, 0:span, LANES:end]
    high_out[...] = high_rim(acc[0, 0:span, 0:LANES], acc[1, 0:span, 0:LANES])
    low_out[...] = low_rim(acc[0, 0:span, end:], acc[1, 0:span, end:])


def second_kernel(
    off, tile, rows, high, low, ch, cl, psi, amp, t, u_out, tile_out, high_out, low_out, ext, acc
):
    p = pl.program_id(0)
    size = psi.shape[2]

    @pl.when(p == 0)
    def _():
        assemble(ext, tile, rows, high, low, ch, cl)
        acc[...] = jnp.zeros_like(acc)

    wr, wi = window(ext, off, p, 0, size), window(ext, off, p, 1, size)
    fr, fi = forward(t, *times(psi[0, 0], psi[0, 1], wr, wi))
    magnitude = jnp.sqrt(fr * fr + fi * fi)
    keep = 1.0 - amp[0] / jnp.maximum(magnitude, 0.5)
    br, bi = inverse(t, fr * keep, fi * keep)
    ur, ui = conj_times(window(ext, off, p, 0, size), window(ext, off, p, 1, size), br, bi)
    u_out[0, 0] = ur
    u_out[0, 1] = ui
    gr, gi = conj_times(psi[0, 0], psi[0, 1], br, bi)
    add_window(acc, off, p, 0, gr)
    add_window(acc, off, p, 1, gi)

    @pl.when(p == pl.num_programs(0) - 1)
    def _():
        leave(acc, tile_out, high_out, low_out, tile_out.shape[1])


def third_kernel(
    off, u, w, probe, prop, t, sum_out, tile_out, high_out, low_out, acc
):
    p = pl.program_id(0)

    @pl.when(p == 0)
    def _():
        acc[...] = jnp.zeros_like(acc)
        sum_out[...] = jnp.zeros_like(sum_out)

    fr, fi = forward(t, u[0, 0], u[0, 1])
    br, bi = inverse(t, *conj_times(prop[0], prop[1], fr, fi))
    sr, si = conj_times(w[0, 0], w[0, 1], br, bi)
    sum_out[0] += sr
    sum_out[1] += si
    gr, gi = conj_times(probe[0], probe[1], br, bi)
    add_window(acc, off, p, 0, gr)
    add_window(acc, off, p, 1, gi)

    @pl.when(p == pl.num_programs(0) - 1)
    def _():
        leave(acc, tile_out, high_out, low_out, tile_out.shape[1])


def merge_kernel(x_ref, from_right, from_left, inner_ref, strip_ref):
    span = x_ref.shape[1]
    size = span - 2 * HALO
    for c in range(2):
        h, w = from_right[...], from_left[...]
        if c:
            h, w = pltpu.roll(h, HALO, 1), pltpu.roll(w, HALO, 1)
        lane = lax.broadcasted_iota(jnp.int32, h.shape, 1)
        h = jnp.where(lane < HALO, 0.0, h)
        w = jnp.where(lane < HALO, w, 0.0)
        full = jnp.concatenate(
            [x_ref[c, :, :LANES] + w, x_ref[c, :, LANES:-LANES], x_ref[c, :, -LANES:] + h], 1
        )
        inner_ref[c] = full[HALO : HALO + size]
        strip_ref[c, 0:HALO] = full[0:HALO]
        strip_ref[c, HALO:] = full[HALO + size :]


def finish_kernel(inner0, strip0, inner1, strip1, out_ref):
    for s, (inner, strip) in enumerate(((inner0, strip0), (inner1, strip1))):
        for c in range(2):
            size = inner.shape[1]
            out_ref[s, c] = inner[c]
            out_ref[s, c, 0:HALO] += strip[c, HALO:]
            out_ref[s, c, size - HALO :] += strip[c, 0:HALO]


def shift(x, axis, by):
    count = lax.axis_size(axis)
    return lax.ppermute(x, axis, [(i, (i + by) % count) for i in range(count)])


def to_both(strips, axis, width, by):
    if lax.axis_size(axis) == 2:
        return shift(strips, axis, 1)
    return jnp.concatenate(
        [shift(strips[:, :width], axis, by), shift(strips[:, width:], axis, -by)], axis=1
    )


def total(x):
    sizes = {axis: lax.axis_size(axis) for axis in ("row", "col")}
    bits = [("col", 1), ("col", 2), ("row", 1)]
    bits = [(axis, bit) for axis, bit in bits if bit < sizes[axis]]
    rest = []
    for axis in ("col", "row"):
        bit = 1
        while bit < sizes[axis]:
            if (axis, bit) not in bits:
                rest.append((axis, bit))
            bit *= 2

    def swap(y, axis, bit):
        return lax.ppermute(y, axis, [(i, i ^ bit) for i in range(sizes[axis])])

    for axis, bit in bits:
        half = x.shape[0] // 2
        upper = lax.axis_index(axis) // bit % 2
        mine = lax.dynamic_slice_in_dim(x, upper * half, half, 0)
        other = lax.dynamic_slice_in_dim(x, (1 - upper) * half, half, 0)
        x = mine + swap(other, axis, bit)
    for axis, bit in rest:
        x = x + swap(x, axis, bit)
    for axis, bit in reversed(bits):
        upper = lax.axis_index(axis) // bit % 2
        other = swap(x, axis, bit)
        x = jnp.where(upper == 0, jnp.concatenate([x, other]), jnp.concatenate([other, x]))
    return x


def local(object_field, offsets, amplitudes, probe, phase):
    tile = object_field.shape[2]
    size = probe.shape[1]
    count = offsets.shape[0]
    off = offsets[:, 0]
    span = tile + 2 * HALO
    ext = pltpu.VMEM((2, span + 8, tile + 2 * LANES), F32)
    t = jnp.asarray(tables(size))
    flops = count * 2 * 4 * 3 * 2 * size**3

    received = []
    for s in range(2):
        edges = jnp.concatenate(
            [object_field[s, :, tile - HALO :], object_field[s, :, :HALO]], axis=1
        )
        received.append(to_both(edges, "row", HALO, 1))
    high, low = rims(object_field)
    high, low = shift(high, "col", 1), shift(low, "col", -1)
    corners = []
    for s in range(2):
        ch, cl = rims(received[s][None])
        corners.append((shift(ch[0], "col", 1), shift(cl[0], "col", -1)))
    prop, amp = prepare(phase, amplitudes[:, 0])

    def block(*shape):
        return pl.BlockSpec((1, *shape), lambda p: (p,) + (0,) * len(shape))

    one = block(2, size, size)
    field = shaped(count, 2, size, size)
    psi, w0 = call(
        first_kernel,
        (field, field),
        flops=flops,
        grid=(count,),
        in_specs=[SMEM] + [VMEM] * 9,
        out_specs=(one, one),
        scratch_shapes=[ext],
    )(off, object_field[0], received[0], high[0], low[0], *corners[0], probe, prop, t)
    left_over = (shaped(2, span, tile), shaped(span, LANES), shaped(span, LANES))
    u, tile1, high1, low1 = call(
        second_kernel,
        (field, *left_over),
        flops=flops,
        grid=(count,),
        in_specs=[SMEM] + [VMEM] * 6 + [one, block(size, size), VMEM],
        out_specs=(one, VMEM, VMEM, VMEM),
        scratch_shapes=[ext, ext],
    )(off, object_field[1], received[1], high[1], low[1], *corners[1], psi, amp, t)
    merge = call(
        merge_kernel,
        (shaped(2, tile, tile), shaped(2, 2 * HALO, tile)),
        in_specs=[VMEM] * 3,
        out_specs=(VMEM, VMEM),
    )
    inner1, strip1 = merge(tile1, shift(high1, "col", -1), shift(low1, "col", 1))
    back1 = to_both(strip1, "row", HALO, -1)
    partial, tile0, high0, low0 = call(
        third_kernel,
        (shaped(2, size, size), *left_over),
        flops=flops,
        grid=(count,),
        in_specs=[SMEM, one, one] + [VMEM] * 3,
        out_specs=(VMEM, VMEM, VMEM, VMEM),
        scratch_shapes=[ext],
    )(off, u, w0, probe, prop, t)
    inner0, strip0 = merge(tile0, shift(high0, "col", -1), shift(low0, "col", 1))
    back0 = to_both(strip0, "row", HALO, -1)
    grad = call(
        finish_kernel,
        shaped(2, 2, tile, tile),
        in_specs=[VMEM] * 4,
        out_specs=VMEM,
    )(inner0, back0, inner1, back1)
    everyone = count * lax.axis_size("row") * lax.axis_size("col")
    summed = total(partial.reshape(2 * size, size)) * (1.0 / math.sqrt(everyone))
    return grad, summed.reshape(2, size, size)


def solution(mesh):
    in_specs = (
        P(None, None, "row", "col"),
        P("row", "col", None),
        P("row", "col", None, None),
        P(),
        P(),
    )
    out_specs = (P(None, None, "row", "col"), P())
    return jax.shard_map(local, mesh=mesh, in_specs=in_specs, out_specs=out_specs, check_vma=False)
```

```python
import functools
import math

import jax
import jax.numpy as jnp
import numpy as np
from jax import lax
from jax.experimental import pallas as pl
from jax.experimental.pallas import tpu as pltpu
from jax.sharding import PartitionSpec as P

HALO = 64
ROOM = 20
CUT_ROOM = 56
PREPARE_ROOM = 56
LANES = 128
F32 = jnp.float32
BF16 = jnp.bfloat16
VMEM = pl.BlockSpec(memory_space=pltpu.VMEM)
SMEM = pl.BlockSpec(memory_space=pltpu.SMEM)


def tables(size):
    half = size // 2
    n = np.arange(half)[:, None]
    k = np.arange(half)[None, :]
    parts = []
    for frequency in (2 * k, 2 * k + 1):
        angle = -2.0 * math.pi * (n * frequency % size) / size
        re, im = np.cos(angle) / math.sqrt(size), np.sin(angle) / math.sqrt(size)
        block = np.block([[re, im], [-im, re]]).astype(np.float32)
        for matrix in (block, block.T):
            high = matrix.astype(jnp.bfloat16)
            low = (matrix - high.astype(np.float32)).astype(jnp.bfloat16)
            parts += [high, low]
    return np.stack(parts)


def split(x):
    high = x.astype(BF16)
    return high, (x - high.astype(F32)).astype(BF16)


def dot(a, b):
    return jnp.dot(a, b, preferred_element_type=F32)


def right(x, t_ref, which):
    high, low = split(x)
    th, tl = t_ref[2 * which], t_ref[2 * which + 1]
    return dot(high, th) + dot(low, th) + dot(high, tl)


def left(t_ref, which, x):
    high, low = split(x)
    th, tl = t_ref[2 * which], t_ref[2 * which + 1]
    return dot(th, high) + dot(th, low) + dot(tl, high)


def forward(t_ref, xr, xi):
    h = xr.shape[0] // 2
    even = right(jnp.concatenate([xr[:, :h] + xr[:, h:], xi[:, :h] + xi[:, h:]], 1), t_ref, 0)
    odd = right(jnp.concatenate([xr[:, :h] - xr[:, h:], xi[:, :h] - xi[:, h:]], 1), t_ref, 2)
    yr = jnp.concatenate([even[:, :h], odd[:, :h]], 1)
    yi = jnp.concatenate([even[:, h:], odd[:, h:]], 1)
    even = left(t_ref, 1, jnp.concatenate([yr[:h] + yr[h:], yi[:h] + yi[h:]], 0))
    odd = left(t_ref, 3, jnp.concatenate([yr[:h] - yr[h:], yi[:h] - yi[h:]], 0))
    zr = jnp.concatenate([even[:h], odd[:h]], 0)
    zi = jnp.concatenate([even[h:], odd[h:]], 0)
    return zr, zi


def inverse(t_ref, zr, zi):
    h = zr.shape[0] // 2
    even = left(t_ref, 0, jnp.concatenate([zr[:h], zi[:h]], 0))
    odd = left(t_ref, 2, jnp.concatenate([zr[h:], zi[h:]], 0))
    p, m = even + odd, even - odd
    yr = jnp.concatenate([p[:h], m[:h]], 0)
    yi = jnp.concatenate([p[h:], m[h:]], 0)
    even = right(jnp.concatenate([yr[:, :h], yi[:, :h]], 1), t_ref, 1)
    odd = right(jnp.concatenate([yr[:, h:], yi[:, h:]], 1), t_ref, 3)
    p, m = even + odd, even - odd
    return jnp.concatenate([p[:, :h], m[:, :h]], 1), jnp.concatenate([p[:, h:], m[:, h:]], 1)


def call(kernel, out_shape, flops=0, room=8, **kwargs):
    return pl.pallas_call(
        kernel,
        out_shape=out_shape,
        cost_estimate=pl.CostEstimate(flops=flops, bytes_accessed=4 << 20, transcendentals=0),
        compiler_params=pltpu.CompilerParams(vmem_limit_bytes=room << 20),
        **kwargs,
    )


def shaped(*shape):
    return jax.ShapeDtypeStruct(shape, F32)


def side_by_side(re, im):
    lane = lax.broadcasted_iota(jnp.int32, re.shape, 1)
    turned = pltpu.roll(im, HALO, 1)
    return lane < HALO, turned


def high_rim(re, im):
    low, turned = side_by_side(re, im)
    return jnp.where(low, turned, re)


def low_rim(re, im):
    low, turned = side_by_side(re, im)
    return jnp.where(low, re, turned)


def cut_kernel(x_ref, *refs):
    slices, _, size, _ = x_ref.shape
    edges, (last, first, columns, sem, col_sem) = refs[:slices], refs[slices:]
    rows, cols = [], []
    for s in range(slices):
        for i, start in enumerate((size - HALO, 0)):
            rows.append(
                pltpu.make_async_copy(
                    x_ref.at[s, :, pl.ds(start, HALO), :],
                    edges[s].at[:, pl.ds(i * HALO, HALO), :],
                    sem.at[s, i],
                )
            )
        for i, start in enumerate((size - LANES, 0)):
            cols.append(
                pltpu.make_async_copy(
                    x_ref.at[s, :, :, pl.ds(start, LANES)], columns.at[s, i], col_sem.at[s, i]
                )
            )
    for copy in cols + rows:
        copy.start()
    for s in range(slices):
        cols[2 * s].wait()
        last[s] = high_rim(columns[s, 0, 0], columns[s, 0, 1])
        cols[2 * s + 1].wait()
        first[s] = low_rim(columns[s, 1, 0], columns[s, 1, 1])
    for copy in rows:
        copy.wait()


def cut(x):
    slices, _, size, _ = x.shape
    rim = shaped(slices, size, LANES)
    outs = (shaped(2, 2 * HALO, size),) * slices + (rim, rim)
    return call(
        cut_kernel,
        outs,
        room=CUT_ROOM,
        in_specs=[pl.BlockSpec(memory_space=pltpu.HBM)],
        out_specs=(VMEM,) * len(outs),
        scratch_shapes=[
            pltpu.VMEM((slices, 2, 2, size, LANES), F32),
            pltpu.SemaphoreType.DMA((slices, 2)),
            pltpu.SemaphoreType.DMA((slices, 2)),
        ],
        name="cut",
    )(x)


def row_corners_kernel(rows_ref, high_ref, low_ref):
    high_ref[...] = high_rim(rows_ref[0, :, -LANES:], rows_ref[1, :, -LANES:])
    low_ref[...] = low_rim(rows_ref[0, :, :LANES], rows_ref[1, :, :LANES])


def row_corners(rows):
    out = shaped(2 * HALO, LANES)
    return call(
        row_corners_kernel, (out, out), in_specs=[VMEM], out_specs=(VMEM, VMEM), name="corners"
    )(rows)


def rim_corners_kernel(s, high_ref, low_ref, out_ref):
    for i, ref in enumerate((high_ref, low_ref)):
        out_ref[i, 0:HALO] = ref[s, -HALO:]
        out_ref[i, HALO:] = ref[s, 0:HALO]


def rim_corners(high, low, s):
    return call(
        functools.partial(rim_corners_kernel, s),
        shaped(2, 2 * HALO, LANES),
        in_specs=[VMEM, VMEM],
        out_specs=VMEM,
        name="corners",
    )(high, low)


def unmixed(x, turned):
    size = x.shape[1]
    half = size // 2
    i = lax.broadcasted_iota(jnp.int32, (size, size), 0)
    j = lax.broadcasted_iota(jnp.int32, (size, size), 1)
    picked = jnp.where(j < half, 2 * j, 2 * (j - half) + 1)
    choose = jnp.where(i == picked, 1.0, 0.0).astype(BF16)
    first = x.astype(BF16)
    rest = x - first.astype(F32)
    second = rest.astype(BF16)
    third = (rest - second.astype(F32)).astype(BF16)
    across = dot(first, choose) + dot(second, choose) + dot(third, choose)
    columns = []
    for k in range(size // LANES):
        turned[k] = across[:, k * LANES : (k + 1) * LANES]
        parts = [turned[k, pl.ds(odd, half, stride=2), :] for odd in (0, 1)]
        columns.append(jnp.concatenate(parts, 0))
    return jnp.concatenate(columns, 1)


def prepare_kernel(phase_ref, amp_ref, prop_ref, out_ref, turned):
    @pl.when(pl.program_id(0) == 0)
    def _():
        phase = unmixed(phase_ref[...], turned)
        prop_ref[0] = jnp.cos(phase)
        prop_ref[1] = jnp.sin(phase)

    out_ref[0] = unmixed(amp_ref[0], turned)


def prepare(phase, amplitudes):
    count, size, _ = amplitudes.shape
    one = pl.BlockSpec((1, size, size), lambda p: (p, 0, 0))
    return call(
        prepare_kernel,
        (shaped(2, size, size), shaped(count, size, size)),
        flops=1 << 29,
        room=PREPARE_ROOM,
        grid=(count,),
        in_specs=[VMEM, one],
        out_specs=(VMEM, one),
        scratch_shapes=[pltpu.VMEM((size // LANES, size, LANES), F32)],
        name="prepare",
    )(phase, amplitudes)


def assemble(ext, tile, rows, high, low, corner_high, corner_low):
    size = tile.shape[2]
    tiles = size // LANES
    spans = ((0, rows, 0, HALO), (HALO, None, 0, size), (HALO + size, rows, HALO, HALO))
    for top, strip, source, length in spans:
        here = pl.ds(top, length)
        there = pl.ds(source, length)
        for c in range(2):
            for j in range(tiles):
                across = slice(j * LANES, (j + 1) * LANES)
                ext[c, j + 1, here] = (
                    tile[0, c, :, across] if strip is None else strip[c, there, across]
                )
        h = high[...] if strip is None else corner_high[there, :]
        w = low[...] if strip is None else corner_low[there, :]
        ext[0, 0, here] = h
        ext[1, 0, here] = pltpu.roll(h, HALO, 1)
        ext[0, tiles + 1, here] = w
        ext[1, tiles + 1, here] = pltpu.roll(w, HALO, 1)


def place(off_ref, p):
    col = off_ref[p, 1] + HALO
    return off_ref[p, 0], col // LANES, col % LANES


def window(ext, off_ref, p, c, size):
    row, tile, turn = place(off_ref, p)
    keep = lax.broadcasted_iota(jnp.int32, (size, LANES), 1) < LANES - turn
    turned = [
        pltpu.roll(ext[c, tile + j, pl.ds(row, size), :], LANES - turn, 1)
        for j in range(size // LANES + 1)
    ]
    return jnp.concatenate(
        [jnp.where(keep, turned[j], turned[j + 1]) for j in range(size // LANES)], 1
    )


def add_window(acc, off_ref, p, c, value):
    size = value.shape[0]
    row, tile, turn = place(off_ref, p)
    keep = lax.broadcasted_iota(jnp.int32, (size, LANES), 1) >= turn
    count = size // LANES
    turned = [pltpu.roll(value[:, j * LANES : (j + 1) * LANES], turn, 1) for j in range(count)]
    zero = jnp.zeros((size, LANES), F32)
    before = [zero] + turned
    after = turned + [zero]
    for j in range(count + 1):
        at = (c, tile + j, pl.ds(row, size))
        acc[at] = acc[at] + jnp.where(keep, after[j], before[j])


def times(ar, ai, br, bi):
    return ar * br - ai * bi, ar * bi + ai * br


def conj_times(ar, ai, br, bi):
    return ar * br + ai * bi, ar * bi - ai * br


def first_kernel(off, tile, rows, high, low, ch, cl, probe, prop, t, psi_out, w_out, ext):
    p = pl.program_id(0)
    size = probe.shape[1]

    @pl.when(p == 0)
    def _():
        assemble(ext, tile, rows, high.at[0], low.at[0], ch, cl)

    wr, wi = window(ext, off, p, 0, size), window(ext, off, p, 1, size)
    w_out[0, 0] = wr
    w_out[0, 1] = wi
    fr, fi = forward(t, *times(probe[0], probe[1], wr, wi))
    xr, xi = inverse(t, *times(prop[0], prop[1], fr, fi))
    psi_out[0, 0] = xr
    psi_out[0, 1] = xi


def leave(acc, tile_out, strip_out, high_out, low_out):
    last = acc.shape[1] - 1
    size = tile_out.shape[1]
    for c in range(2):
        for j in range(1, last):
            across = slice((j - 1) * LANES, j * LANES)
            tile_out[c, :, across] = acc[c, j, HALO : HALO + size]
            strip_out[c, 0:HALO, across] = acc[c, j, 0:HALO]
            strip_out[c, HALO:, across] = acc[c, j, HALO + size :]
    high_out[...] = high_rim(acc[0, 0], acc[1, 0])
    low_out[...] = low_rim(acc[0, last], acc[1, last])


def second_kernel(
    off, tile, rows, high, low, corners, psi, amp, t, u_out, tile_out, strip_out, high_out, low_out, ext, acc
):
    p = pl.program_id(0)
    size = psi.shape[2]

    @pl.when(p == 0)
    def _():
        assemble(ext, tile, rows, high.at[1], low.at[1], corners.at[0], corners.at[1])
        acc[...] = jnp.zeros_like(acc)

    wr, wi = window(ext, off, p, 0, size), window(ext, off, p, 1, size)
    fr, fi = forward(t, *times(psi[0, 0], psi[0, 1], wr, wi))
    magnitude = jnp.sqrt(fr * fr + fi * fi)
    keep = 1.0 - amp[0] / jnp.maximum(magnitude, 0.5)
    br, bi = inverse(t, fr * keep, fi * keep)
    ur, ui = conj_times(window(ext, off, p, 0, size), window(ext, off, p, 1, size), br, bi)
    u_out[0, 0] = ur
    u_out[0, 1] = ui
    gr, gi = conj_times(psi[0, 0], psi[0, 1], br, bi)
    add_window(acc, off, p, 0, gr)
    add_window(acc, off, p, 1, gi)

    @pl.when(p == pl.num_programs(0) - 1)
    def _():
        leave(acc, tile_out, strip_out, high_out, low_out)


def third_kernel(up, u, w, prop, t, beta_out, mine_out, other_out, acc):
    p = pl.program_id(0)

    @pl.when(p == 0)
    def _():
        acc[...] = jnp.zeros_like(acc)

    fr, fi = forward(t, u[0, 0], u[0, 1])
    br, bi = inverse(t, *conj_times(prop[0], prop[1], fr, fi))
    beta_out[0, 0] = br
    beta_out[0, 1] = bi
    sr, si = conj_times(w[0, 0], w[0, 1], br, bi)
    acc[0] += sr
    acc[1] += si

    @pl.when(p == pl.num_programs(0) - 1)
    def _():
        mine_out[...] = acc[up[0]]
        other_out[...] = acc[1 - up[0]]


def spread_kernel(off, beta, probe, tile_out, strip_out, high_out, low_out, acc):
    p = pl.program_id(0)

    @pl.when(p == 0)
    def _():
        acc[...] = jnp.zeros_like(acc)

    gr, gi = conj_times(probe[0], probe[1], beta[0, 0], beta[0, 1])
    add_window(acc, off, p, 0, gr)
    add_window(acc, off, p, 1, gi)

    @pl.when(p == pl.num_programs(0) - 1)
    def _():
        leave(acc, tile_out, strip_out, high_out, low_out)


def rim_parts(from_right, from_left, c):
    h, w = from_right, from_left
    if c:
        h, w = pltpu.roll(h, HALO, 1), pltpu.roll(w, HALO, 1)
    lane = lax.broadcasted_iota(jnp.int32, h.shape, 1)
    return jnp.where(lane < HALO, 0.0, h), jnp.where(lane < HALO, w, 0.0)


def merge_kernel(x_ref, from_right, from_left, strip_ref):
    end = from_right.shape[0] - HALO
    for c in range(2):
        for i, start in enumerate((0, end)):
            here = pl.ds(i * HALO, HALO)
            h, w = rim_parts(from_right[pl.ds(start, HALO)], from_left[pl.ds(start, HALO)], c)
            strip_ref[c, here, :LANES] = x_ref[c, here, :LANES] + w
            strip_ref[c, here, LANES:-LANES] = x_ref[c, here, LANES:-LANES]
            strip_ref[c, here, -LANES:] = x_ref[c, here, -LANES:] + h


def finish_kernel(*refs):
    out_ref = refs[-1]
    size = out_ref.shape[2]
    for s in range(out_ref.shape[0]):
        inner, from_right, from_left, strip = refs[4 * s : 4 * s + 4]
        middle = pl.ds(HALO, size)
        for c in range(2):
            h, w = rim_parts(from_right[middle], from_left[middle], c)
            out_ref[s, c, :, :LANES] = inner[c, :, :LANES] + w
            out_ref[s, c, :, LANES:-LANES] = inner[c, :, LANES:-LANES]
            out_ref[s, c, :, -LANES:] = inner[c, :, -LANES:] + h
            out_ref[s, c, 0:HALO] += strip[c, HALO:]
            out_ref[s, c, size - HALO :] += strip[c, 0:HALO]


def shift(x, axis, by):
    count = lax.axis_size(axis)
    return lax.ppermute(x, axis, [(i, (i + by) % count) for i in range(count)])


def to_both(strips, axis, width, by):
    if lax.axis_size(axis) == 2:
        return shift(strips, axis, 1)
    return jnp.concatenate(
        [shift(strips[:, :width], axis, by), shift(strips[:, width:], axis, -by)], axis=1
    )


def halving_kernel(at, up, mine, came, mine_out, other_out):
    half = mine_out.shape[0]
    here = pl.ds(pl.multiple_of(up[at] * half, half), half)
    there = pl.ds(pl.multiple_of((1 - up[at]) * half, half), half)
    mine_out[...] = mine[here] + came[here]
    other_out[...] = mine[there] + came[there]


def adding_kernel(mine, came, out):
    out[...] = mine[...] + came[...]


def joining_kernel(at, factor, up, mine, came, out):
    half = mine.shape[0]
    out[pl.ds(pl.multiple_of(up[at] * half, half), half)] = mine[...] * factor
    out[pl.ds(pl.multiple_of((1 - up[at]) * half, half), half)] = came[...] * factor


def halvings():
    return [("col", bit) for bit in (1, 2, 4) if bit < lax.axis_size("col")]


def sides():
    return jnp.stack([lax.axis_index(axis) // bit % 2 for axis, bit in halvings()])


def total(up, mine, other, factor):
    sizes = {axis: lax.axis_size(axis) for axis in ("row", "col")}
    halves = halvings()
    rest = []
    for axis in ("row", "col"):
        bit = 1
        while bit < sizes[axis]:
            if (axis, bit) not in halves:
                rest.append((axis, bit))
            bit *= 2

    def swap(y, axis, bit):
        return lax.ppermute(y, axis, [(i, i ^ bit) for i in range(sizes[axis])])

    def add(x, came):
        return call(
            adding_kernel, shaped(*x.shape), in_specs=[VMEM] * 2, out_specs=VMEM, name="adding"
        )(x, came)

    for at, (axis, bit) in enumerate(halves):
        came = swap(other, axis, bit)
        if at + 1 == len(halves):
            x = add(mine, came)
            break
        out = shaped(mine.shape[0] // 2, mine.shape[1])
        mine, other = call(
            functools.partial(halving_kernel, at + 1),
            (out, out),
            in_specs=[SMEM, VMEM, VMEM],
            out_specs=(VMEM, VMEM),
            name="halving",
        )(up, mine, came)
    for axis, bit in rest:
        x = add(x, swap(x, axis, bit))
    for at, (axis, bit) in reversed(list(enumerate(halves))):
        x = call(
            functools.partial(joining_kernel, at, 1.0 if at else factor),
            shaped(2 * x.shape[0], x.shape[1]),
            in_specs=[SMEM, VMEM, VMEM],
            out_specs=VMEM,
            name="joining",
        )(up, x, swap(x, axis, bit))
    return x


def local(object_field, offsets, amplitudes, probe, phase):
    tile = object_field.shape[2]
    size = probe.shape[1]
    count = offsets.shape[0]
    off = offsets[:, 0]
    span = tile + 2 * HALO
    ext = pltpu.VMEM((2, tile // LANES + 2, span, LANES), F32)
    t = jnp.asarray(tables(size))
    flops = count * 2 * 4 * 3 * 2 * size**3

    up = sides()
    edges0, edges1, last, first = cut(object_field)
    rows0 = to_both(edges0, "row", HALO, 1)
    high = shift(last, "col", 1)
    low = shift(first, "col", -1)
    prop, amp = prepare(phase, amplitudes[:, 0])
    rows1 = to_both(edges1, "row", HALO, 1)
    corner_high, corner_low = row_corners(rows0)
    corner_high = shift(corner_high, "col", 1)
    corner_low = shift(corner_low, "col", -1)
    corners1 = rim_corners(high, low, 1)
    corners1 = to_both(corners1, "row", HALO, 1)

    def block(*shape):
        return pl.BlockSpec((1, *shape), lambda p: (p,) + (0,) * len(shape))

    def slice_of(s):
        return pl.BlockSpec((1, 2, tile, tile), lambda p: (s, 0, 0, 0), pipeline_mode=pl.Buffered(1))

    one = block(2, size, size)
    field = shaped(count, 2, size, size)
    psi, w0 = call(
        first_kernel,
        (field, field),
        flops=flops,
        room=ROOM,
        grid=(count,),
        in_specs=[SMEM, slice_of(0)] + [VMEM] * 8,
        out_specs=(one, one),
        scratch_shapes=[ext],
        name="first",
    )(off, object_field, rows0, high, low, corner_high, corner_low, probe, prop, t)
    left_over = (
        shaped(2, tile, tile),
        shaped(2, 2 * HALO, tile),
        shaped(span, LANES),
        shaped(span, LANES),
    )
    u, tile1, strip1, high1, low1 = call(
        second_kernel,
        (field, *left_over),
        flops=flops,
        room=ROOM,
        grid=(count,),
        in_specs=[SMEM, slice_of(1)] + [VMEM] * 4 + [one, block(size, size), VMEM],
        out_specs=(one, VMEM, VMEM, VMEM, VMEM),
        scratch_shapes=[ext, ext],
        name="second",
    )(off, object_field, rows1, high, low, corners1, psi, amp, t)
    right1 = shift(high1, "col", -1)
    left1 = shift(low1, "col", 1)
    beta, mine, other = call(
        third_kernel,
        (field, shaped(size, size), shaped(size, size)),
        flops=flops,
        room=ROOM,
        grid=(count,),
        in_specs=[SMEM, one, one, VMEM, VMEM],
        out_specs=(one, VMEM, VMEM),
        scratch_shapes=[pltpu.VMEM((2, size, size), F32)],
        name="third",
    )(up, u, w0, prop, t)
    tile0, strip0, high0, low0 = call(
        spread_kernel,
        left_over,
        room=ROOM,
        grid=(count,),
        in_specs=[SMEM, one, VMEM],
        out_specs=(VMEM,) * 4,
        scratch_shapes=[ext],
        name="spread",
    )(off, beta, probe)
    merge = call(
        merge_kernel,
        shaped(2, 2 * HALO, tile),
        in_specs=[VMEM] * 3,
        out_specs=VMEM,
        name="merge",
    )
    strip1 = merge(strip1, right1, left1)
    back1 = to_both(strip1, "row", HALO, -1)
    right0 = shift(high0, "col", -1)
    left0 = shift(low0, "col", 1)
    strip0 = merge(strip0, right0, left0)
    back0 = to_both(strip0, "row", HALO, -1)
    grad = call(
        finish_kernel,
        shaped(2, 2, tile, tile),
        room=16,
        in_specs=[VMEM] * 8,
        out_specs=VMEM,
        name="finish",
    )(tile0, right0, left0, back0, tile1, right1, left1, back1)
    everyone = count * lax.axis_size("row") * lax.axis_size("col")
    summed = total(up, mine, other, 1.0 / math.sqrt(everyone))
    return grad, summed.reshape(2, size, size)


def solution(mesh):
    in_specs = (
        P(None, None, "row", "col"),
        P("row", "col", None),
        P("row", "col", None, None),
        P(),
        P(),
    )
    out_specs = (P(None, None, "row", "col"), P())

    return jax.shard_map(local, mesh=mesh, in_specs=in_specs, out_specs=out_specs, check_vma=False)
```

```python
import functools
import math

import jax
import jax.numpy as jnp
from jax import lax
from jax.experimental import pallas as pl
from jax.experimental.pallas import tpu as pltpu
from jax.sharding import PartitionSpec as P

HALO = 64
ROOM = 20
CUT_ROOM = 61
LANES = 128
F32 = jnp.float32
BF16 = jnp.bfloat16
VMEM = pl.BlockSpec(memory_space=pltpu.VMEM)
SMEM = pl.BlockSpec(memory_space=pltpu.SMEM)


def split(x):
    high = x.astype(BF16)
    return high, (x - high.astype(F32)).astype(BF16)


def dot(a, b):
    return jnp.dot(a, b, preferred_element_type=F32)


class Stage:
    def __init__(self, t, high, low, product):
        self.t, self.high, self.low, self.product = t, high, low, product
        self.group = range(high.shape[0])
        self.half = high.shape[2] // 2

    def put(self, q, e, x):
        self.high[q, e], self.low[q, e] = split(x)

    def right(self, q, e, which):
        th, tl = self.t[2 * which], self.t[2 * which + 1]
        high, low = self.high[q, e], self.low[q, e]
        return dot(high, th) + dot(low, th) + dot(high, tl)

    def left(self, q, e, which):
        th, tl = self.t[2 * which], self.t[2 * which + 1]
        high, low = self.high[q, e], self.low[q, e]
        return dot(th, high) + dot(th, low) + dot(tl, high)

    def forward(self, source):
        h = self.half
        for q in self.group:
            x = source(q)
            self.put(q, 0, jnp.concatenate([y[:, :h] + y[:, h:] for y in x], 1))
            self.put(q, 1, jnp.concatenate([y[:, :h] - y[:, h:] for y in x], 1))
        for q in self.group:
            self.product[q, 0] = self.right(q, 0, 0)
            self.product[q, 1] = self.right(q, 1, 2)
        for q in self.group:
            top = self.product[q, :, :h, :]
            bottom = self.product[q, :, h:, :]
            for e, y in enumerate((top + bottom, top - bottom)):
                parts = [
                    jnp.concatenate([y[k, :, c * h : (c + 1) * h] for k in (0, 1)], 1) for c in (0, 1)
                ]
                self.put(q, e, jnp.concatenate(parts, 0))
        for q in self.group:
            self.product[q, 0] = self.left(q, 0, 1)
            self.product[q, 1] = self.left(q, 1, 3)

    def inverse(self, change, sink):
        h = self.half
        for q in self.group:
            for e in (0, 1):
                z = change(q, e, self.product[q, e, :h], self.product[q, e, h:])
                self.put(q, e, jnp.concatenate(z, 0))
        for q in self.group:
            self.product[q, 0] = self.left(q, 0, 0)
            self.product[q, 1] = self.left(q, 1, 2)
        for q in self.group:
            even, odd = self.product[q, 0], self.product[q, 1]
            p, m = even + odd, even - odd
            parts = [jnp.concatenate([p[c * h : (c + 1) * h], m[c * h : (c + 1) * h]], 0) for c in (0, 1)]
            self.put(q, 0, jnp.concatenate([y[:, :h] for y in parts], 1))
            self.put(q, 1, jnp.concatenate([y[:, h:] for y in parts], 1))
        for q in self.group:
            even, odd = self.right(q, 0, 1), self.right(q, 1, 3)
            p, m = even + odd, even - odd
            sink(q, *[jnp.concatenate([y[:, c * h : (c + 1) * h] for y in (p, m)], 1) for c in (0, 1)])


def group_of(count):
    return 2 if count % 2 == 0 else 1


def stage_scratch(count, size):
    shape = (group_of(count), 2, size, size)
    return [pltpu.VMEM(shape, BF16), pltpu.VMEM(shape, BF16), pltpu.VMEM(shape, F32)]


def call(kernel, out_shape, flops=0, room=8, **kwargs):
    return pl.pallas_call(
        kernel,
        out_shape=out_shape,
        cost_estimate=pl.CostEstimate(flops=flops, bytes_accessed=4 << 20, transcendentals=0),
        compiler_params=pltpu.CompilerParams(vmem_limit_bytes=room << 20),
        **kwargs,
    )


def shaped(*shape):
    return jax.ShapeDtypeStruct(shape, F32)


def side_by_side(re, im):
    lane = lax.broadcasted_iota(jnp.int32, re.shape, 1)
    turned = pltpu.roll(im, HALO, 1)
    return lane < HALO, turned


def high_rim(re, im):
    low, turned = side_by_side(re, im)
    return jnp.where(low, turned, re)


def low_rim(re, im):
    low, turned = side_by_side(re, im)
    return jnp.where(low, re, turned)


def upper(at):
    axis, bit = halvings()[at]
    return lax.axis_index(axis) // bit % 2


def on_odd():
    return lax.axis_index("col") % 2 == 1


def swapped(odd, a, b):
    return jnp.where(odd, b, a), jnp.where(odd, a, b)


def row_copies(x_ref, s, out, sem):
    size = x_ref.shape[2]
    return [
        pltpu.make_async_copy(
            x_ref.at[s, :, pl.ds(start, HALO), :], out.at[:, pl.ds(i * HALO, HALO), :], sem.at[i]
        )
        for i, start in enumerate((size - HALO, 0))
    ]


def cut_rows_kernel(s, x_ref, out, sem):
    copies = row_copies(x_ref, s, out, sem)
    for copy in copies:
        copy.start()
    for copy in copies:
        copy.wait()


def cut_rows(x, s):
    size = x.shape[2]
    return call(
        functools.partial(cut_rows_kernel, s),
        shaped(2, 2 * HALO, size),
        room=CUT_ROOM + 1,
        in_specs=[pl.BlockSpec(memory_space=pltpu.HBM)],
        out_specs=VMEM,
        scratch_shapes=[pltpu.SemaphoreType.DMA((2,))],
        name="cut",
    )(x)


def cut_kernel(off, x_ref, edge, near, far, columns, sem, col_sem):
    odd = on_odd()
    slices, _, size, _ = x_ref.shape
    rows = row_copies(x_ref, slices - 1, edge, sem)
    cols = [
        pltpu.make_async_copy(
            x_ref.at[s, :, :, pl.ds(start, LANES)], columns.at[s, i], col_sem.at[s, i]
        )
        for s in range(slices)
        for i, start in enumerate((size - LANES, 0))
    ]
    for copy in cols + rows:
        copy.start()
    for s in range(slices):
        cols[2 * s].wait()
        cols[2 * s + 1].wait()
        near[s], far[s] = swapped(
            odd,
            high_rim(columns[s, 0, 0], columns[s, 0, 1]),
            low_rim(columns[s, 1, 0], columns[s, 1, 1]),
        )
    for copy in rows:
        copy.wait()


def cut(off, x):
    slices, _, size, _ = x.shape
    rim = shaped(slices, size, LANES)
    return call(
        cut_kernel,
        (shaped(2, 2 * HALO, size), rim, rim),
        room=CUT_ROOM,
        in_specs=[SMEM, pl.BlockSpec(memory_space=pltpu.HBM)],
        out_specs=(VMEM,) * 3,
        scratch_shapes=[
            pltpu.VMEM((slices, 2, 2, size, LANES), F32),
            pltpu.SemaphoreType.DMA((2,)),
            pltpu.SemaphoreType.DMA((slices, 2)),
        ],
        name="cut",
    )(off, x)


def row_corners_kernel(rows_ref, near, far):
    near[...], far[...] = swapped(
        on_odd(),
        high_rim(rows_ref[0, :, -LANES:], rows_ref[1, :, -LANES:]),
        low_rim(rows_ref[0, :, :LANES], rows_ref[1, :, :LANES]),
    )


def row_corners(rows):
    out = shaped(2 * HALO, LANES)
    return call(
        row_corners_kernel,
        (out, out),
        in_specs=[VMEM],
        out_specs=(VMEM, VMEM),
        name="corners",
    )(rows)


def rim_corners_kernel(s, near, far, out_ref):
    for i, ref in enumerate((near, far)):
        out_ref[i, 0:HALO] = ref[s, -HALO:]
        out_ref[i, HALO:] = ref[s, 0:HALO]


def rim_corners(near, far, s):
    return call(
        functools.partial(rim_corners_kernel, s),
        shaped(2, 2 * HALO, LANES),
        in_specs=[VMEM, VMEM],
        out_specs=VMEM,
        name="corners",
    )(near, far)


def chooser(size):
    half = size // 2
    i = lax.broadcasted_iota(jnp.int32, (size, size), 0)
    j = lax.broadcasted_iota(jnp.int32, (size, size), 1)
    picked = jnp.where(j < half, 2 * j, 2 * (j - half) + 1)
    return jnp.where(i == picked, 1.0, 0.0).astype(BF16)


def unmixed(across, turned):
    size = across.shape[1]
    for k in range(size // LANES):
        turned[k] = across[:, k * LANES : (k + 1) * LANES]
    rows = []
    for odd in (0, 1):
        here = pl.ds(odd, across.shape[0] // 2, stride=2)
        rows.append(jnp.concatenate([turned[k, here, :] for k in range(size // LANES)], 1))
    return jnp.concatenate(rows, 0)


def write_tables(t_out):
    size = t_out.shape[1]
    half = size // 2
    i = lax.broadcasted_iota(jnp.int32, (half, half), 0)
    j = lax.broadcasted_iota(jnp.int32, (half, half), 1)
    products = (2 * i * j, 2 * j * i, i * (2 * j + 1), j * (2 * i + 1))
    for which, product in enumerate(products):
        angle = (product % size).astype(F32) * (2.0 * math.pi / size)
        re = jnp.cos(angle) * (1.0 / math.sqrt(size))
        im = jnp.sin(angle) * (-1.0 / math.sqrt(size))
        if which % 2:
            im = -im
        for r, row in enumerate(((re, im), (-im, re))):
            for c, part in enumerate(row):
                at = (slice(r * half, (r + 1) * half), slice(c * half, (c + 1) * half))
                t_out[(2 * which, *at)], t_out[(2 * which + 1, *at)] = split(part)


def prepare_kernel(phase_ref, prop_ref, t_out, turned):
    write_tables(t_out)
    x = phase_ref[...]
    choose = chooser(x.shape[0])
    first, rest = split(x)
    third = (x - first.astype(F32) - rest.astype(F32)).astype(BF16)
    phase = unmixed(dot(first, choose) + dot(rest, choose) + dot(third, choose), turned)
    prop_ref[0] = jnp.cos(phase)
    prop_ref[1] = jnp.sin(phase)


def prepare(phase):
    size = phase.shape[0]
    return call(
        prepare_kernel,
        (shaped(2, size, size), jax.ShapeDtypeStruct((8, size, size), BF16)),
        flops=1 << 28,
        in_specs=[VMEM],
        out_specs=(VMEM, VMEM),
        scratch_shapes=[pltpu.VMEM((size // LANES, size, LANES), F32)],
        name="prepare",
    )(phase)


def assemble(ext, tile, rows, near, far, corner_near, corner_far, odd):
    size = tile.shape[1]
    tiles = size // LANES
    spans = ((0, rows, 0, HALO), (HALO, None, 0, size), (HALO + size, rows, HALO, HALO))
    for top, strip, source, length in spans:
        here = pl.ds(top, length)
        there = pl.ds(source, length)
        for c in range(2):
            for j in range(tiles):
                across = slice(j * LANES, (j + 1) * LANES)
                ext[c, j + 1, here] = (
                    tile[c, :, across] if strip is None else strip[c, there, across]
                )
        w, h = swapped(
            odd,
            near[...] if strip is None else corner_near[there, :],
            far[...] if strip is None else corner_far[there, :],
        )
        ext[0, 0, here] = h
        ext[1, 0, here] = pltpu.roll(h, HALO, 1)
        ext[0, tiles + 1, here] = w
        ext[1, tiles + 1, here] = pltpu.roll(w, HALO, 1)


def place(off_ref, p):
    col = off_ref[p, 1] + HALO
    return off_ref[p, 0], col // LANES, col % LANES


def window(ext, off_ref, p, c, size):
    row, tile, turn = place(off_ref, p)
    keep = lax.broadcasted_iota(jnp.int32, (size, LANES), 1) < LANES - turn
    turned = [
        pltpu.roll(ext[c, tile + j, pl.ds(row, size), :], LANES - turn, 1)
        for j in range(size // LANES + 1)
    ]
    return jnp.concatenate(
        [jnp.where(keep, turned[j], turned[j + 1]) for j in range(size // LANES)], 1
    )


def add_window(acc, off_ref, p, c, value):
    size = value.shape[0]
    row, tile, turn = place(off_ref, p)
    keep = lax.broadcasted_iota(jnp.int32, (size, LANES), 1) >= turn
    count = size // LANES
    turned = [pltpu.roll(value[:, j * LANES : (j + 1) * LANES], turn, 1) for j in range(count)]
    zero = jnp.zeros((size, LANES), F32)
    before = [zero] + turned
    after = turned + [zero]
    for j in range(count + 1):
        at = (c, tile + j, pl.ds(row, size))
        acc[at] = acc[at] + jnp.where(keep, after[j], before[j])


def times(ar, ai, br, bi):
    return ar * br - ai * bi, ar * bi + ai * br


def conj_times(ar, ai, br, bi):
    return ar * br + ai * bi, ar * bi - ai * br


def first_kernel(off, x, rows, near, far, cn, cf, probe, prop, t, psi_out, w_out, ext, *buffers):
    stage = Stage(t, *buffers)
    count, _, size, _ = psi_out.shape
    many = len(stage.group)
    h = stage.half
    assemble(ext, x.at[0], rows, near.at[0], far.at[0], cn, cf, on_odd())

    @pl.loop(0, count // many)
    def _(i):
        first = i * many

        def source(q):
            w = [window(ext, off, first + q, c, size) for c in (0, 1)]
            w_out[first + q, 0], w_out[first + q, 1] = w
            return times(probe[0], probe[1], *w)

        def change(q, e, re, im):
            here = slice(e * h, (e + 1) * h)
            return times(prop[0, here], prop[1, here], re, im)

        def sink(q, re, im):
            psi_out[first + q, 0], psi_out[first + q, 1] = re, im

        stage.forward(source)
        stage.inverse(change, sink)


def leave(acc, near, far, odd):
    last = acc.shape[1] - 1
    near[...], far[...] = swapped(
        odd, low_rim(acc[0, last], acc[1, last]), high_rim(acc[0, 0], acc[1, 0])
    )


def second_kernel(
    off,
    x,
    rows,
    near,
    far,
    corners,
    psi,
    amp,
    t,
    u_out,
    acc,
    near_out,
    far_out,
    ext,
    kept,
    choose,
    turned,
    level,
    *buffers,
):
    stage = Stage(t, *buffers)
    count, _, size, _ = psi.shape
    many = len(stage.group)
    h = stage.half
    odd = on_odd()
    assemble(ext, x.at[1], rows, near.at[1], far.at[1], corners.at[0], corners.at[1], odd)
    acc[...] = jnp.zeros_like(acc)
    choose[...] = chooser(size)

    @pl.loop(0, count // many)
    def _(i):
        first = i * many
        for q in stage.group:
            top, rest = split(amp[first + q])
            level[q] = unmixed(dot(top, choose[...]) + dot(rest, choose[...]), turned.at[q])

        def source(q):
            w = [window(ext, off, first + q, c, size) for c in (0, 1)]
            kept[q, 0], kept[q, 1] = w
            return times(psi[first + q, 0], psi[first + q, 1], *w)

        def change(q, e, re, im):
            magnitude = jnp.sqrt(re * re + im * im)
            keep = 1.0 - level[q, e * h : (e + 1) * h] / jnp.maximum(magnitude, 0.5)
            return re * keep, im * keep

        def sink(q, re, im):
            p = first + q
            u_out[p, 0], u_out[p, 1] = conj_times(kept[q, 0], kept[q, 1], re, im)
            for c, g in enumerate(conj_times(psi[p, 0], psi[p, 1], re, im)):
                add_window(acc, off, p, c, g)

        stage.forward(source)
        stage.inverse(change, sink)

    leave(acc, near_out, far_out, odd)


def third_kernel(factor, u, w, prop, t, beta_out, mine_out, other_out, acc, *buffers):
    stage = Stage(t, *buffers)
    count = u.shape[0]
    many = len(stage.group)
    h = stage.half
    acc[...] = jnp.zeros_like(acc)

    @pl.loop(0, count // many)
    def _(i):
        first = i * many

        def source(q):
            return u[first + q, 0], u[first + q, 1]

        def change(q, e, re, im):
            here = slice(e * h, (e + 1) * h)
            return conj_times(prop[0, here], prop[1, here], re, im)

        def sink(q, re, im):
            p = first + q
            beta_out[p, 0], beta_out[p, 1] = re, im
            for c, g in enumerate(conj_times(w[p, 0], w[p, 1], re, im)):
                acc[c] += g

        stage.forward(source)
        stage.inverse(change, sink)

    mine_out[...] = acc[upper(0)] * factor
    other_out[...] = acc[1 - upper(0)] * factor


def spread_kernel(off, beta, probe, acc, near_out, far_out):
    acc[...] = jnp.zeros_like(acc)

    @pl.loop(0, beta.shape[0])
    def _(p):
        for c, g in enumerate(conj_times(probe[0], probe[1], beta[p, 0], beta[p, 1])):
            add_window(acc, off, p, c, g)

    leave(acc, near_out, far_out, on_odd())


def rim_parts(near, far, odd, c):
    h, w = swapped(odd, near, far)
    if c:
        h, w = pltpu.roll(h, HALO, 1), pltpu.roll(w, HALO, 1)
    lane = lax.broadcasted_iota(jnp.int32, h.shape, 1)
    return jnp.where(lane < HALO, 0.0, h), jnp.where(lane < HALO, w, 0.0)


def merge_kernel(acc, near, far, strip_ref):
    tiles = acc.shape[1] - 2
    end = near.shape[0] - HALO
    for c in range(2):
        for i, start in enumerate((0, end)):
            here, there = pl.ds(i * HALO, HALO), pl.ds(start, HALO)
            h, w = rim_parts(near[there], far[there], on_odd(), c)
            for j in range(tiles):
                value = acc[c, j + 1, there]
                if j == 0:
                    value += w
                if j == tiles - 1:
                    value += h
                strip_ref[c, here, j * LANES : (j + 1) * LANES] = value


def finish_kernel(*refs):
    out_ref = refs[-1]
    size = out_ref.shape[2]
    tiles = size // LANES
    middle = pl.ds(HALO, size)
    for s in range(out_ref.shape[0]):
        acc, near, far, strip = refs[4 * s : 4 * s + 4]
        for c in range(2):
            h, w = rim_parts(near[middle], far[middle], on_odd(), c)
            for j in range(tiles):
                value = acc[c, j + 1, middle]
                if j == 0:
                    value += w
                if j == tiles - 1:
                    value += h
                across = slice(j * LANES, (j + 1) * LANES)
                out_ref[s, c, HALO:-HALO, across] = value[HALO:-HALO]
                out_ref[s, c, :HALO, across] = value[:HALO] + strip[c, HALO:, across]
                out_ref[s, c, -HALO:, across] = value[-HALO:] + strip[c, :HALO, across]


def shift(x, axis, by):
    count = lax.axis_size(axis)
    return lax.ppermute(x, axis, [(i, (i + by) % count) for i in range(count)])


def exchange(near, far):
    count = lax.axis_size("col")
    near = lax.ppermute(near, "col", [(i, i ^ 1) for i in range(count)])
    far = lax.ppermute(far, "col", [(i, (i + i % 2 * 2 - 1) % count) for i in range(count)])
    return near, far


def to_both(strips, axis, width, by):
    if lax.axis_size(axis) == 2:
        return shift(strips, axis, 1)
    return jnp.concatenate(
        [shift(strips[:, :width], axis, by), shift(strips[:, width:], axis, -by)], axis=1
    )


def halving_kernel(at, mine, came, mine_out, other_out):
    half = mine_out.shape[0]
    here = pl.ds(pl.multiple_of(upper(at) * half, half), half)
    there = pl.ds(pl.multiple_of((1 - upper(at)) * half, half), half)
    mine_out[...] = mine[here] + came[here]
    other_out[...] = mine[there] + came[there]


def adding_kernel(mine, came, out):
    out[...] = mine[...] + came[...]


def joining_kernel(at, mine, came, out):
    half = mine.shape[0]
    out[pl.ds(pl.multiple_of(upper(at) * half, half), half)] = mine[...]
    out[pl.ds(pl.multiple_of((1 - upper(at)) * half, half), half)] = came[...]


def ending_kernel(mine, came, out, sem):
    copies = [
        pltpu.make_async_copy(mine, out.at[upper(0)], sem.at[0]),
        pltpu.make_async_copy(came, out.at[1 - upper(0)], sem.at[1]),
    ]
    for copy in copies:
        copy.start()
    for copy in copies:
        copy.wait()


def halvings():
    return [("col", bit) for bit in (1, 2, 4) if bit < lax.axis_size("col")]


def total(mine, other):
    sizes = {axis: lax.axis_size(axis) for axis in ("row", "col")}
    halves = halvings()
    rest = []
    for axis in ("row", "col"):
        bit = 1
        while bit < sizes[axis]:
            if (axis, bit) not in halves:
                rest.append((axis, bit))
            bit *= 2

    def swap(y, axis, bit):
        return lax.ppermute(y, axis, [(i, i ^ bit) for i in range(sizes[axis])])

    def add(x, came):
        return call(
            adding_kernel, shaped(*x.shape), in_specs=[VMEM] * 2, out_specs=VMEM, name="adding"
        )(x, came)

    for at, (axis, bit) in enumerate(halves):
        came = swap(other, axis, bit)
        if at + 1 == len(halves):
            x = add(mine, came)
            break
        out = shaped(mine.shape[0] // 2, mine.shape[1])
        mine, other = call(
            functools.partial(halving_kernel, at + 1),
            (out, out),
            in_specs=[VMEM, VMEM],
            out_specs=(VMEM, VMEM),
            name="halving",
        )(mine, came)
    for axis, bit in rest:
        x = add(x, swap(x, axis, bit))
    for at, (axis, bit) in reversed(list(enumerate(halves))):
        came = swap(x, axis, bit)
        if at == 0:
            return call(
                ending_kernel,
                shaped(2, *x.shape),
                in_specs=[VMEM, VMEM],
                out_specs=pl.BlockSpec(memory_space=pltpu.HBM),
                scratch_shapes=[pltpu.SemaphoreType.DMA((2,))],
                name="ending",
            )(x, came)
        x = call(
            functools.partial(joining_kernel, at),
            shaped(2 * x.shape[0], x.shape[1]),
            in_specs=[VMEM, VMEM],
            out_specs=VMEM,
            name="joining",
        )(x, came)


def local(object_field, offsets, amplitudes, probe, phase):
    tile = object_field.shape[2]
    size = probe.shape[1]
    count = offsets.shape[0]
    off = offsets[:, 0]
    span = tile + 2 * HALO
    ext = pltpu.VMEM((2, tile // LANES + 2, span, LANES), F32)
    flops = count * 2 * 4 * 3 * 2 * size**3

    edges0 = cut_rows(object_field, 0)
    edges1, near, far = cut(off, object_field)
    rows0 = to_both(edges0, "row", HALO, 1)
    near, far = exchange(near, far)
    prop, t = prepare(phase)
    rows1 = to_both(edges1, "row", HALO, 1)
    corner_near, corner_far = row_corners(rows0)
    corner_near, corner_far = exchange(corner_near, corner_far)
    corners1 = rim_corners(near, far, 1)
    corners1 = to_both(corners1, "row", HALO, 1)

    field = shaped(count, 2, size, size)
    buffers = stage_scratch(count, size)
    many = group_of(count)
    everyone = count * lax.axis_size("row") * lax.axis_size("col")
    factor = 1.0 / math.sqrt(everyone)
    psi, w0 = call(
        first_kernel,
        (field, field),
        flops=flops,
        room=ROOM,
        in_specs=[SMEM] + [VMEM] * 9,
        out_specs=(VMEM,) * 2,
        scratch_shapes=[ext, *buffers],
        name="first",
    )(off, object_field, rows0, near, far, corner_near, corner_far, probe, prop, t)
    left_over = (shaped(*ext.shape), shaped(span, LANES), shaped(span, LANES))
    u, sum1, near1, far1 = call(
        second_kernel,
        (field, *left_over),
        flops=flops,
        room=ROOM,
        in_specs=[SMEM] + [VMEM] * 8,
        out_specs=(VMEM,) * 4,
        scratch_shapes=[
            ext,
            pltpu.VMEM((many, 2, size, size), F32),
            pltpu.VMEM((size, size), BF16),
            pltpu.VMEM((many, size // LANES, size, LANES), F32),
            pltpu.VMEM((many, size, size), F32),
            *buffers,
        ],
        name="second",
    )(off, object_field, rows1, near, far, corners1, psi, amplitudes[:, 0], t)
    near1, far1 = exchange(near1, far1)
    beta, mine, other = call(
        functools.partial(third_kernel, factor),
        (field, shaped(size, size), shaped(size, size)),
        flops=flops,
        room=ROOM,
        in_specs=[VMEM] * 4,
        out_specs=(VMEM,) * 3,
        scratch_shapes=[pltpu.VMEM((2, size, size), F32), *buffers],
        name="third",
    )(u, w0, prop, t)
    sum0, near0, far0 = call(
        spread_kernel,
        left_over,
        room=ROOM,
        in_specs=[SMEM] + [VMEM] * 2,
        out_specs=(VMEM,) * 3,
        name="spread",
    )(off, beta, probe)
    near0, far0 = exchange(near0, far0)
    merge = call(
        merge_kernel,
        shaped(2, 2 * HALO, tile),
        in_specs=[VMEM] * 3,
        out_specs=VMEM,
        name="merge",
    )
    strip1 = merge(sum1, near1, far1)
    back1 = to_both(strip1, "row", HALO, -1)
    strip0 = merge(sum0, near0, far0)
    back0 = to_both(strip0, "row", HALO, -1)
    grad = call(
        finish_kernel,
        shaped(2, 2, tile, tile),
        room=16,
        in_specs=[VMEM] * 8,
        out_specs=VMEM,
        name="finish",
    )(sum0, near0, far0, back0, sum1, near1, far1, back1)
    return grad, total(mine, other)


def solution(mesh):
    in_specs = (
        P(None, None, "row", "col"),
        P("row", "col", None),
        P("row", "col", None, None),
        P(),
        P(),
    )
    out_specs = (P(None, None, "row", "col"), P())

    return jax.shard_map(local, mesh=mesh, in_specs=in_specs, out_specs=out_specs, check_vma=False)
```

```python
import functools
import math

import jax
import jax.numpy as jnp
from jax import lax
from jax.experimental import pallas as pl
from jax.experimental.pallas import tpu as pltpu
from jax.sharding import PartitionSpec as P

HALO = 64
ROOM = 20
LANES = 128
F32 = jnp.float32
BF16 = jnp.bfloat16
VMEM = pl.BlockSpec(memory_space=pltpu.VMEM)
SMEM = pl.BlockSpec(memory_space=pltpu.SMEM)


def split(x):
    high = x.astype(BF16)
    return high, (x - high.astype(F32)).astype(BF16)


def dot(a, b):
    return jnp.dot(a, b, preferred_element_type=F32)


class Stage:
    def __init__(self, t, high, low, product):
        self.t, self.high, self.low, self.product = t, high, low, product
        self.group = range(high.shape[0])
        self.half = high.shape[2] // 2

    def put(self, q, e, x):
        self.high[q, e], self.low[q, e] = split(x)

    def right(self, q, e, which):
        th, tl = self.t[2 * which], self.t[2 * which + 1]
        high, low = self.high[q, e], self.low[q, e]
        return dot(high, th) + dot(low, th) + dot(high, tl)

    def left(self, q, e, which):
        th, tl = self.t[2 * which], self.t[2 * which + 1]
        high, low = self.high[q, e], self.low[q, e]
        return dot(th, high) + dot(th, low) + dot(tl, high)

    def forward(self, source):
        h = self.half
        for q in self.group:
            x = source(q)
            self.put(q, 0, jnp.concatenate([y[:, :h] + y[:, h:] for y in x], 1))
            self.put(q, 1, jnp.concatenate([y[:, :h] - y[:, h:] for y in x], 1))
        for q in self.group:
            self.product[q, 0] = self.right(q, 0, 0)
            self.product[q, 1] = self.right(q, 1, 2)
        for q in self.group:
            top = self.product[q, :, :h, :]
            bottom = self.product[q, :, h:, :]
            for e, y in enumerate((top + bottom, top - bottom)):
                parts = [
                    jnp.concatenate([y[k, :, c * h : (c + 1) * h] for k in (0, 1)], 1) for c in (0, 1)
                ]
                self.put(q, e, jnp.concatenate(parts, 0))
        for q in self.group:
            self.product[q, 0] = self.left(q, 0, 1)
            self.product[q, 1] = self.left(q, 1, 3)

    def inverse(self, change, sink):
        h = self.half
        for q in self.group:
            for e in (0, 1):
                z = change(q, e, self.product[q, e, :h], self.product[q, e, h:])
                self.put(q, e, jnp.concatenate(z, 0))
        for q in self.group:
            self.product[q, 0] = self.left(q, 0, 0)
            self.product[q, 1] = self.left(q, 1, 2)
        for q in self.group:
            even, odd = self.product[q, 0], self.product[q, 1]
            p, m = even + odd, even - odd
            parts = [jnp.concatenate([p[c * h : (c + 1) * h], m[c * h : (c + 1) * h]], 0) for c in (0, 1)]
            self.put(q, 0, jnp.concatenate([y[:, :h] for y in parts], 1))
            self.put(q, 1, jnp.concatenate([y[:, h:] for y in parts], 1))
        for q in self.group:
            even, odd = self.right(q, 0, 1), self.right(q, 1, 3)
            p, m = even + odd, even - odd
            sink(q, *[jnp.concatenate([y[:, c * h : (c + 1) * h] for y in (p, m)], 1) for c in (0, 1)])


def group_of(count):
    return 2 if count % 2 == 0 else 1


def stage_scratch(count, size):
    shape = (group_of(count), 2, size, size)
    return [pltpu.VMEM(shape, BF16), pltpu.VMEM(shape, BF16), pltpu.VMEM(shape, F32)]


def call(kernel, out_shape, flops=0, room=8, **kwargs):
    return pl.pallas_call(
        kernel,
        out_shape=out_shape,
        cost_estimate=pl.CostEstimate(flops=flops, bytes_accessed=4 << 20, transcendentals=0),
        compiler_params=pltpu.CompilerParams(vmem_limit_bytes=room << 20),
        **kwargs,
    )


def shaped(*shape):
    return jax.ShapeDtypeStruct(shape, F32)


def side_by_side(re, im):
    lane = lax.broadcasted_iota(jnp.int32, re.shape, 1)
    turned = pltpu.roll(im, HALO, 1)
    return lane < HALO, turned


def high_rim(re, im):
    low, turned = side_by_side(re, im)
    return jnp.where(low, turned, re)


def low_rim(re, im):
    low, turned = side_by_side(re, im)
    return jnp.where(low, re, turned)


def upper(at):
    axis, bit = halvings()[at]
    return lax.axis_index(axis) // bit % 2


def on_odd():
    return lax.axis_index("col") % 2 == 1


def swapped(odd, a, b):
    return jnp.where(odd, b, a), jnp.where(odd, a, b)


def cut_rows_kernel(s, x_ref, out):
    size = x_ref.shape[2]
    for c in range(2):
        out[c, :HALO] = x_ref[s, c, size - HALO :]
        out[c, HALO:] = x_ref[s, c, :HALO]


def cut_rows(x, s):
    return call(
        functools.partial(cut_rows_kernel, s),
        shaped(2, 2 * HALO, x.shape[2]),
        in_specs=[VMEM],
        out_specs=VMEM,
        name="cut",
    )(x)


def cut_kernel(x_ref, near, far):
    for s in range(x_ref.shape[0]):
        near[s], far[s] = swapped(
            on_odd(),
            high_rim(x_ref[s, 0, :, -LANES:], x_ref[s, 1, :, -LANES:]),
            low_rim(x_ref[s, 0, :, :LANES], x_ref[s, 1, :, :LANES]),
        )


def cut(x):
    slices, _, size, _ = x.shape
    rim = shaped(slices, size, LANES)
    return call(
        cut_kernel, (rim, rim), in_specs=[VMEM], out_specs=(VMEM,) * 2, name="cut"
    )(x)


def row_corners_kernel(rows_ref, near, far):
    near[...], far[...] = swapped(
        on_odd(),
        high_rim(rows_ref[0, :, -LANES:], rows_ref[1, :, -LANES:]),
        low_rim(rows_ref[0, :, :LANES], rows_ref[1, :, :LANES]),
    )


def row_corners(rows):
    out = shaped(2 * HALO, LANES)
    return call(
        row_corners_kernel,
        (out, out),
        in_specs=[VMEM],
        out_specs=(VMEM, VMEM),
        name="corners",
    )(rows)


def rim_corners_kernel(s, near, far, out_ref):
    for i, ref in enumerate((near, far)):
        out_ref[i, 0:HALO] = ref[s, -HALO:]
        out_ref[i, HALO:] = ref[s, 0:HALO]


def rim_corners(near, far, s):
    return call(
        functools.partial(rim_corners_kernel, s),
        shaped(2, 2 * HALO, LANES),
        in_specs=[VMEM, VMEM],
        out_specs=VMEM,
        name="corners",
    )(near, far)


def chooser(size):
    half = size // 2
    i = lax.broadcasted_iota(jnp.int32, (size, size), 0)
    j = lax.broadcasted_iota(jnp.int32, (size, size), 1)
    picked = jnp.where(j < half, 2 * j, 2 * (j - half) + 1)
    return jnp.where(i == picked, 1.0, 0.0).astype(BF16)


def unmixed(across, turned):
    size = across.shape[1]
    for k in range(size // LANES):
        turned[k] = across[:, k * LANES : (k + 1) * LANES]
    rows = []
    for odd in (0, 1):
        here = pl.ds(odd, across.shape[0] // 2, stride=2)
        rows.append(jnp.concatenate([turned[k, here, :] for k in range(size // LANES)], 1))
    return jnp.concatenate(rows, 0)


def write_tables(t_out):
    size = t_out.shape[1]
    half = size // 2
    i = lax.broadcasted_iota(jnp.int32, (half, half), 0)
    j = lax.broadcasted_iota(jnp.int32, (half, half), 1)
    products = (2 * i * j, 2 * j * i, i * (2 * j + 1), j * (2 * i + 1))
    for which, product in enumerate(products):
        angle = (product % size).astype(F32) * (2.0 * math.pi / size)
        re = jnp.cos(angle) * (1.0 / math.sqrt(size))
        im = jnp.sin(angle) * (-1.0 / math.sqrt(size))
        if which % 2:
            im = -im
        for r, row in enumerate(((re, im), (-im, re))):
            for c, part in enumerate(row):
                at = (slice(r * half, (r + 1) * half), slice(c * half, (c + 1) * half))
                t_out[(2 * which, *at)], t_out[(2 * which + 1, *at)] = split(part)


def prepare_kernel(phase_ref, prop_ref, t_out, turned):
    write_tables(t_out)
    x = phase_ref[...]
    choose = chooser(x.shape[0])
    first, rest = split(x)
    third = (x - first.astype(F32) - rest.astype(F32)).astype(BF16)
    phase = unmixed(dot(first, choose) + dot(rest, choose) + dot(third, choose), turned)
    prop_ref[0] = jnp.cos(phase)
    prop_ref[1] = jnp.sin(phase)


def prepare(phase):
    size = phase.shape[0]
    return call(
        prepare_kernel,
        (shaped(2, size, size), jax.ShapeDtypeStruct((8, size, size), BF16)),
        flops=1 << 28,
        in_specs=[VMEM],
        out_specs=(VMEM, VMEM),
        scratch_shapes=[pltpu.VMEM((size // LANES, size, LANES), F32)],
        name="prepare",
    )(phase)


def assemble(ext, tile, rows, near, far, corner_near, corner_far, odd):
    size = tile.shape[1]
    tiles = size // LANES
    spans = ((0, rows, 0, HALO), (HALO, None, 0, size), (HALO + size, rows, HALO, HALO))
    for top, strip, source, length in spans:
        here = pl.ds(top, length)
        there = pl.ds(source, length)
        for c in range(2):
            for j in range(tiles):
                across = slice(j * LANES, (j + 1) * LANES)
                ext[c, j + 1, here] = (
                    tile[c, :, across] if strip is None else strip[c, there, across]
                )
        w, h = swapped(
            odd,
            near[...] if strip is None else corner_near[there, :],
            far[...] if strip is None else corner_far[there, :],
        )
        ext[0, 0, here] = h
        ext[1, 0, here] = pltpu.roll(h, HALO, 1)
        ext[0, tiles + 1, here] = w
        ext[1, tiles + 1, here] = pltpu.roll(w, HALO, 1)


def place(off_ref, p):
    col = off_ref[1, p] + HALO
    return off_ref[0, p], col // LANES, col % LANES


def window(ext, off_ref, p, c, size):
    row, tile, turn = place(off_ref, p)
    keep = lax.broadcasted_iota(jnp.int32, (size, LANES), 1) < LANES - turn
    turned = [
        pltpu.roll(ext[c, tile + j, pl.ds(row, size), :], LANES - turn, 1)
        for j in range(size // LANES + 1)
    ]
    return jnp.concatenate(
        [jnp.where(keep, turned[j], turned[j + 1]) for j in range(size // LANES)], 1
    )


def add_window(acc, off_ref, p, c, value):
    size = value.shape[0]
    row, tile, turn = place(off_ref, p)
    keep = lax.broadcasted_iota(jnp.int32, (size, LANES), 1) >= turn
    count = size // LANES
    turned = [pltpu.roll(value[:, j * LANES : (j + 1) * LANES], turn, 1) for j in range(count)]
    zero = jnp.zeros((size, LANES), F32)
    before = [zero] + turned
    after = turned + [zero]
    for j in range(count + 1):
        at = (c, tile + j, pl.ds(row, size))
        acc[at] = acc[at] + jnp.where(keep, after[j], before[j])


def times(ar, ai, br, bi):
    return ar * br - ai * bi, ar * bi + ai * br


def conj_times(ar, ai, br, bi):
    return ar * br + ai * bi, ar * bi - ai * br


def first_kernel(off, x, rows, near, far, cn, cf, probe, prop, t, psi_out, w_out, ext, *buffers):
    stage = Stage(t, *buffers)
    count, _, size, _ = psi_out.shape
    many = len(stage.group)
    h = stage.half
    assemble(ext, x.at[0], rows, near.at[0], far.at[0], cn, cf, on_odd())

    @pl.loop(0, count // many)
    def _(i):
        first = i * many

        def source(q):
            w = [window(ext, off, first + q, c, size) for c in (0, 1)]
            w_out[first + q, 0], w_out[first + q, 1] = w
            return times(probe[0], probe[1], *w)

        def change(q, e, re, im):
            here = slice(e * h, (e + 1) * h)
            return times(prop[0, here], prop[1, here], re, im)

        def sink(q, re, im):
            psi_out[first + q, 0], psi_out[first + q, 1] = re, im

        stage.forward(source)
        stage.inverse(change, sink)


def leave(acc, near, far, odd):
    last = acc.shape[1] - 1
    near[...], far[...] = swapped(
        odd, low_rim(acc[0, last], acc[1, last]), high_rim(acc[0, 0], acc[1, 0])
    )


def second_kernel(
    off,
    x,
    rows,
    near,
    far,
    corners,
    psi,
    amp,
    t,
    u_out,
    acc,
    near_out,
    far_out,
    ext,
    kept,
    choose,
    turned,
    level,
    *buffers,
):
    stage = Stage(t, *buffers)
    count, _, size, _ = psi.shape
    many = len(stage.group)
    h = stage.half
    odd = on_odd()
    assemble(ext, x.at[1], rows, near.at[1], far.at[1], corners.at[0], corners.at[1], odd)
    acc[...] = jnp.zeros_like(acc)
    choose[...] = chooser(size)

    @pl.loop(0, count // many)
    def _(i):
        first = i * many
        for q in stage.group:
            top, rest = split(amp[first + q])
            level[q] = unmixed(dot(top, choose[...]) + dot(rest, choose[...]), turned.at[q])

        def source(q):
            w = [window(ext, off, first + q, c, size) for c in (0, 1)]
            kept[q, 0], kept[q, 1] = w
            return times(psi[first + q, 0], psi[first + q, 1], *w)

        def change(q, e, re, im):
            magnitude = jnp.sqrt(re * re + im * im)
            keep = 1.0 - level[q, e * h : (e + 1) * h] / jnp.maximum(magnitude, 0.5)
            return re * keep, im * keep

        def sink(q, re, im):
            p = first + q
            u_out[p, 0], u_out[p, 1] = conj_times(kept[q, 0], kept[q, 1], re, im)
            for c, g in enumerate(conj_times(psi[p, 0], psi[p, 1], re, im)):
                add_window(acc, off, p, c, g)

        stage.forward(source)
        stage.inverse(change, sink)

    leave(acc, near_out, far_out, odd)


def third_kernel(factor, u, w, prop, t, beta_out, mine_out, other_out, acc, *buffers):
    stage = Stage(t, *buffers)
    count = u.shape[0]
    many = len(stage.group)
    h = stage.half
    acc[...] = jnp.zeros_like(acc)

    @pl.loop(0, count // many)
    def _(i):
        first = i * many

        def source(q):
            return u[first + q, 0], u[first + q, 1]

        def change(q, e, re, im):
            here = slice(e * h, (e + 1) * h)
            return conj_times(prop[0, here], prop[1, here], re, im)

        def sink(q, re, im):
            p = first + q
            beta_out[p, 0], beta_out[p, 1] = re, im
            for c, g in enumerate(conj_times(w[p, 0], w[p, 1], re, im)):
                acc[c] += g

        stage.forward(source)
        stage.inverse(change, sink)

    mine_out[...] = acc[upper(0)] * factor
    other_out[...] = acc[1 - upper(0)] * factor


def spread_kernel(off, beta, probe, acc, near_out, far_out):
    acc[...] = jnp.zeros_like(acc)

    @pl.loop(0, beta.shape[0])
    def _(p):
        for c, g in enumerate(conj_times(probe[0], probe[1], beta[p, 0], beta[p, 1])):
            add_window(acc, off, p, c, g)

    leave(acc, near_out, far_out, on_odd())


def rim_parts(near, far, odd, c):
    h, w = swapped(odd, near, far)
    if c:
        h, w = pltpu.roll(h, HALO, 1), pltpu.roll(w, HALO, 1)
    lane = lax.broadcasted_iota(jnp.int32, h.shape, 1)
    return jnp.where(lane < HALO, 0.0, h), jnp.where(lane < HALO, w, 0.0)


def merge_kernel(acc, near, far, strip_ref):
    tiles = acc.shape[1] - 2
    end = near.shape[0] - HALO
    for c in range(2):
        for i, start in enumerate((0, end)):
            here, there = pl.ds(i * HALO, HALO), pl.ds(start, HALO)
            h, w = rim_parts(near[there], far[there], on_odd(), c)
            for j in range(tiles):
                value = acc[c, j + 1, there]
                if j == 0:
                    value += w
                if j == tiles - 1:
                    value += h
                strip_ref[c, here, j * LANES : (j + 1) * LANES] = value


def finish_kernel(*refs):
    out_ref = refs[-1]
    size = out_ref.shape[2]
    tiles = size // LANES
    middle = pl.ds(HALO, size)
    for s in range(out_ref.shape[0]):
        acc, near, far, strip = refs[4 * s : 4 * s + 4]
        for c in range(2):
            h, w = rim_parts(near[middle], far[middle], on_odd(), c)
            for j in range(tiles):
                value = acc[c, j + 1, middle]
                if j == 0:
                    value += w
                if j == tiles - 1:
                    value += h
                across = slice(j * LANES, (j + 1) * LANES)
                out_ref[s, c, HALO:-HALO, across] = value[HALO:-HALO]
                out_ref[s, c, :HALO, across] = value[:HALO] + strip[c, HALO:, across]
                out_ref[s, c, -HALO:, across] = value[-HALO:] + strip[c, :HALO, across]


def shift(x, axis, by):
    count = lax.axis_size(axis)
    return lax.ppermute(x, axis, [(i, (i + by) % count) for i in range(count)])


def exchange(near, far):
    count = lax.axis_size("col")
    far = lax.ppermute(far, "col", [(i, (i + i % 2 * 2 - 1) % count) for i in range(count)])
    near = lax.ppermute(near, "col", [(i, i ^ 1) for i in range(count)])
    return near, far


def to_both(strips, axis, width, by):
    if lax.axis_size(axis) == 2:
        return shift(strips, axis, 1)
    return jnp.concatenate(
        [shift(strips[:, :width], axis, by), shift(strips[:, width:], axis, -by)], axis=1
    )


def halving_kernel(at, mine, came, mine_out, other_out):
    half = mine_out.shape[0]
    here = pl.ds(pl.multiple_of(upper(at) * half, half), half)
    there = pl.ds(pl.multiple_of((1 - upper(at)) * half, half), half)
    mine_out[...] = mine[here] + came[here]
    other_out[...] = mine[there] + came[there]


def adding_kernel(mine, came, out):
    out[...] = mine[...] + came[...]


def joining_kernel(at, mine, came, out):
    half = mine.shape[0]
    out[pl.ds(pl.multiple_of(upper(at) * half, half), half)] = mine[...]
    out[pl.ds(pl.multiple_of((1 - upper(at)) * half, half), half)] = came[...]


def ending_kernel(mine, came, out, sem):
    copies = [
        pltpu.make_async_copy(mine, out.at[upper(0)], sem.at[0]),
        pltpu.make_async_copy(came, out.at[1 - upper(0)], sem.at[1]),
    ]
    for copy in copies:
        copy.start()
    for copy in copies:
        copy.wait()


def halvings():
    return [("col", bit) for bit in (1, 2, 4) if bit < lax.axis_size("col")]


def total(mine, other):
    sizes = {axis: lax.axis_size(axis) for axis in ("row", "col")}
    halves = halvings()
    rest = []
    for axis in ("row", "col"):
        bit = 1
        while bit < sizes[axis]:
            if (axis, bit) not in halves:
                rest.append((axis, bit))
            bit *= 2

    def swap(y, axis, bit):
        return lax.ppermute(y, axis, [(i, i ^ bit) for i in range(sizes[axis])])

    def add(x, came):
        return call(
            adding_kernel, shaped(*x.shape), in_specs=[VMEM] * 2, out_specs=VMEM, name="adding"
        )(x, came)

    for at, (axis, bit) in enumerate(halves):
        came = swap(other, axis, bit)
        if at + 1 == len(halves):
            x = add(mine, came)
            break
        out = shaped(mine.shape[0] // 2, mine.shape[1])
        mine, other = call(
            functools.partial(halving_kernel, at + 1),
            (out, out),
            in_specs=[VMEM, VMEM],
            out_specs=(VMEM, VMEM),
            name="halving",
        )(mine, came)
    for axis, bit in rest:
        x = add(x, swap(x, axis, bit))
    for at, (axis, bit) in reversed(list(enumerate(halves))):
        came = swap(x, axis, bit)
        if at == 0:
            return call(
                ending_kernel,
                shaped(2, *x.shape),
                in_specs=[VMEM, VMEM],
                out_specs=pl.BlockSpec(memory_space=pltpu.HBM),
                scratch_shapes=[pltpu.SemaphoreType.DMA((2,))],
                name="ending",
            )(x, came)
        x = call(
            functools.partial(joining_kernel, at),
            shaped(2 * x.shape[0], x.shape[1]),
            in_specs=[VMEM, VMEM],
            out_specs=VMEM,
            name="joining",
        )(x, came)


def local(object_field, offsets, amplitudes, probe, phase):
    tile = object_field.shape[2]
    size = probe.shape[1]
    count = offsets.shape[0]
    off = jnp.transpose(offsets[:, 0])
    span = tile + 2 * HALO
    ext = pltpu.VMEM((2, tile // LANES + 2, span, LANES), F32)
    flops = count * 2 * 4 * 3 * 2 * size**3

    edges0 = cut_rows(object_field, 0)
    near, far = cut(object_field)
    edges1 = cut_rows(object_field, 1)
    rows0 = to_both(edges0, "row", HALO, 1)
    near, far = exchange(near, far)
    prop, t = prepare(phase)
    rows1 = to_both(edges1, "row", HALO, 1)
    corner_near, corner_far = row_corners(rows0)
    corner_near, corner_far = exchange(corner_near, corner_far)
    corners1 = rim_corners(near, far, 1)
    corners1 = to_both(corners1, "row", HALO, 1)

    field = shaped(count, 2, size, size)
    buffers = stage_scratch(count, size)
    many = group_of(count)
    everyone = count * lax.axis_size("row") * lax.axis_size("col")
    factor = 1.0 / math.sqrt(everyone)
    psi, w0 = call(
        first_kernel,
        (field, field),
        flops=flops,
        room=ROOM,
        in_specs=[SMEM] + [VMEM] * 9,
        out_specs=(VMEM,) * 2,
        scratch_shapes=[ext, *buffers],
        name="first",
    )(off, object_field, rows0, near, far, corner_near, corner_far, probe, prop, t)
    left_over = (shaped(*ext.shape), shaped(span, LANES), shaped(span, LANES))
    u, sum1, near1, far1 = call(
        second_kernel,
        (field, *left_over),
        flops=flops,
        room=ROOM,
        in_specs=[SMEM] + [VMEM] * 8,
        out_specs=(VMEM,) * 4,
        scratch_shapes=[
            ext,
            pltpu.VMEM((many, 2, size, size), F32),
            pltpu.VMEM((size, size), BF16),
            pltpu.VMEM((many, size // LANES, size, LANES), F32),
            pltpu.VMEM((many, size, size), F32),
            *buffers,
        ],
        name="second",
    )(off, object_field, rows1, near, far, corners1, psi, amplitudes[:, 0], t)
    near1, far1 = exchange(near1, far1)
    beta, mine, other = call(
        functools.partial(third_kernel, factor),
        (field, shaped(size, size), shaped(size, size)),
        flops=flops,
        room=ROOM,
        in_specs=[VMEM] * 4,
        out_specs=(VMEM,) * 3,
        scratch_shapes=[pltpu.VMEM((2, size, size), F32), *buffers],
        name="third",
    )(u, w0, prop, t)
    sum0, near0, far0 = call(
        spread_kernel,
        left_over,
        room=ROOM,
        in_specs=[SMEM] + [VMEM] * 2,
        out_specs=(VMEM,) * 3,
        name="spread",
    )(off, beta, probe)
    near0, far0 = exchange(near0, far0)
    merge = call(
        merge_kernel,
        shaped(2, 2 * HALO, tile),
        in_specs=[VMEM] * 3,
        out_specs=VMEM,
        name="merge",
    )
    strip1 = merge(sum1, near1, far1)
    back1 = to_both(strip1, "row", HALO, -1)
    strip0 = merge(sum0, near0, far0)
    back0 = to_both(strip0, "row", HALO, -1)
    grad = call(
        finish_kernel,
        shaped(2, 2, tile, tile),
        room=16,
        in_specs=[VMEM] * 8,
        out_specs=VMEM,
        name="finish",
    )(sum0, near0, far0, back0, sum1, near1, far1, back1)
    return grad, total(mine, other)


def solution(mesh):
    in_specs = (
        P(None, None, "row", "col"),
        P("row", "col", None),
        P("row", "col", None, None),
        P(),
        P(),
    )
    out_specs = (P(None, None, "row", "col"), P())

    return jax.shard_map(local, mesh=mesh, in_specs=in_specs, out_specs=out_specs, check_vma=False)
```

```python
import functools
import math

import jax
import jax.numpy as jnp
from jax import lax
from jax.experimental import pallas as pl
from jax.experimental.pallas import tpu as pltpu
from jax.sharding import PartitionSpec as P

HALO = 64
ROOM = 20
LANES = 128
F32 = jnp.float32
BF16 = jnp.bfloat16
VMEM = pl.BlockSpec(memory_space=pltpu.VMEM)
SMEM = pl.BlockSpec(memory_space=pltpu.SMEM)


def split(x):
    high = x.astype(BF16)
    return high, (x - high.astype(F32)).astype(BF16)


def dot(a, b):
    return jnp.dot(a, b, preferred_element_type=F32)


class Stage:
    def __init__(self, t, high, low, product):
        self.t, self.high, self.low, self.product = t, high, low, product
        self.group = range(high.shape[0])
        self.half = high.shape[2] // 2

    def put(self, q, e, x):
        self.high[q, e], self.low[q, e] = split(x)

    def right(self, q, e, which):
        th, tl = self.t[2 * which], self.t[2 * which + 1]
        high, low = self.high[q, e], self.low[q, e]
        return dot(high, th) + dot(low, th) + dot(high, tl)

    def left(self, q, e, which):
        th, tl = self.t[2 * which], self.t[2 * which + 1]
        high, low = self.high[q, e], self.low[q, e]
        return dot(th, high) + dot(th, low) + dot(tl, high)

    def forward(self, source):
        h = self.half
        for q in self.group:
            x = source(q)
            self.put(q, 0, jnp.concatenate([y[:, :h] + y[:, h:] for y in x], 1))
            self.put(q, 1, jnp.concatenate([y[:, :h] - y[:, h:] for y in x], 1))
        for q in self.group:
            self.product[q, 0] = self.right(q, 0, 0)
            self.product[q, 1] = self.right(q, 1, 2)
        for q in self.group:
            top = self.product[q, :, :h, :]
            bottom = self.product[q, :, h:, :]
            for e, y in enumerate((top + bottom, top - bottom)):
                parts = [
                    jnp.concatenate([y[k, :, c * h : (c + 1) * h] for k in (0, 1)], 1) for c in (0, 1)
                ]
                self.put(q, e, jnp.concatenate(parts, 0))
        for q in self.group:
            self.product[q, 0] = self.left(q, 0, 1)
            self.product[q, 1] = self.left(q, 1, 3)

    def inverse(self, change, sink):
        h = self.half
        for q in self.group:
            for e in (0, 1):
                z = change(q, e, self.product[q, e, :h], self.product[q, e, h:])
                self.put(q, e, jnp.concatenate(z, 0))
        for q in self.group:
            self.product[q, 0] = self.left(q, 0, 0)
            self.product[q, 1] = self.left(q, 1, 2)
        for q in self.group:
            even, odd = self.product[q, 0], self.product[q, 1]
            p, m = even + odd, even - odd
            parts = [jnp.concatenate([p[c * h : (c + 1) * h], m[c * h : (c + 1) * h]], 0) for c in (0, 1)]
            self.put(q, 0, jnp.concatenate([y[:, :h] for y in parts], 1))
            self.put(q, 1, jnp.concatenate([y[:, h:] for y in parts], 1))
        for q in self.group:
            even, odd = self.right(q, 0, 1), self.right(q, 1, 3)
            p, m = even + odd, even - odd
            sink(q, *[jnp.concatenate([y[:, c * h : (c + 1) * h] for y in (p, m)], 1) for c in (0, 1)])


def group_of(count):
    return 2 if count % 2 == 0 else 1


def stage_scratch(count, size):
    shape = (group_of(count), 2, size, size)
    return [pltpu.VMEM(shape, BF16), pltpu.VMEM(shape, BF16), pltpu.VMEM(shape, F32)]


def call(kernel, out_shape, flops=0, room=8, **kwargs):
    return pl.pallas_call(
        kernel,
        out_shape=out_shape,
        cost_estimate=pl.CostEstimate(flops=flops, bytes_accessed=4 << 20, transcendentals=0),
        compiler_params=pltpu.CompilerParams(vmem_limit_bytes=room << 20),
        **kwargs,
    )


def shaped(*shape):
    return jax.ShapeDtypeStruct(shape, F32)


def side_by_side(re, im):
    lane = lax.broadcasted_iota(jnp.int32, re.shape, 1)
    turned = pltpu.roll(im, HALO, 1)
    return lane < HALO, turned


def high_rim(re, im):
    low, turned = side_by_side(re, im)
    return jnp.where(low, turned, re)


def low_rim(re, im):
    low, turned = side_by_side(re, im)
    return jnp.where(low, re, turned)


def upper(at):
    axis, bit = halvings()[at]
    return lax.axis_index(axis) // bit % 2


def on_odd():
    return lax.axis_index("col") % 2 == 1


def swapped(odd, a, b):
    return jnp.where(odd, b, a), jnp.where(odd, a, b)


def cut_rows_kernel(s, x_ref, out):
    size = x_ref.shape[2]
    for c in range(2):
        out[c, :HALO] = x_ref[s, c, size - HALO :]
        out[c, HALO:] = x_ref[s, c, :HALO]


def cut_rows(x, s):
    return call(
        functools.partial(cut_rows_kernel, s),
        shaped(2, 2 * HALO, x.shape[2]),
        in_specs=[VMEM],
        out_specs=VMEM,
        name="cut",
    )(x)


def cut_kernel(x_ref, near, far):
    for s in range(x_ref.shape[0]):
        near[s], far[s] = swapped(
            on_odd(),
            high_rim(x_ref[s, 0, :, -LANES:], x_ref[s, 1, :, -LANES:]),
            low_rim(x_ref[s, 0, :, :LANES], x_ref[s, 1, :, :LANES]),
        )


def cut(x):
    slices, _, size, _ = x.shape
    rim = shaped(slices, size, LANES)
    return call(
        cut_kernel, (rim, rim), in_specs=[VMEM], out_specs=(VMEM,) * 2, name="cut"
    )(x)


def row_corners_kernel(rows_ref, near, far):
    near[...], far[...] = swapped(
        on_odd(),
        high_rim(rows_ref[0, :, -LANES:], rows_ref[1, :, -LANES:]),
        low_rim(rows_ref[0, :, :LANES], rows_ref[1, :, :LANES]),
    )


def row_corners(rows):
    out = shaped(2 * HALO, LANES)
    return call(
        row_corners_kernel,
        (out, out),
        in_specs=[VMEM],
        out_specs=(VMEM, VMEM),
        name="corners",
    )(rows)


def rim_corners_kernel(s, near, far, out_ref):
    for i, ref in enumerate((near, far)):
        out_ref[i, 0:HALO] = ref[s, -HALO:]
        out_ref[i, HALO:] = ref[s, 0:HALO]


def rim_corners(near, far, s):
    return call(
        functools.partial(rim_corners_kernel, s),
        shaped(2, 2 * HALO, LANES),
        in_specs=[VMEM, VMEM],
        out_specs=VMEM,
        name="corners",
    )(near, far)


def chooser(size):
    half = size // 2
    i = lax.broadcasted_iota(jnp.int32, (size, size), 0)
    j = lax.broadcasted_iota(jnp.int32, (size, size), 1)
    picked = jnp.where(j < half, 2 * j, 2 * (j - half) + 1)
    return jnp.where(i == picked, 1.0, 0.0).astype(BF16)


def unmixed(across, turned):
    size = across.shape[1]
    for k in range(size // LANES):
        turned[k] = across[:, k * LANES : (k + 1) * LANES]
    rows = []
    for odd in (0, 1):
        here = pl.ds(odd, across.shape[0] // 2, stride=2)
        rows.append(jnp.concatenate([turned[k, here, :] for k in range(size // LANES)], 1))
    return jnp.concatenate(rows, 0)


def write_tables(t_out):
    size = t_out.shape[1]
    half = size // 2
    i = lax.broadcasted_iota(jnp.int32, (half, half), 0)
    j = lax.broadcasted_iota(jnp.int32, (half, half), 1)
    products = (2 * i * j, 2 * j * i, i * (2 * j + 1), j * (2 * i + 1))
    for which, product in enumerate(products):
        angle = (product % size).astype(F32) * (2.0 * math.pi / size)
        re = jnp.cos(angle) * (1.0 / math.sqrt(size))
        im = jnp.sin(angle) * (-1.0 / math.sqrt(size))
        if which % 2:
            im = -im
        for r, row in enumerate(((re, im), (-im, re))):
            for c, part in enumerate(row):
                at = (slice(r * half, (r + 1) * half), slice(c * half, (c + 1) * half))
                t_out[(2 * which, *at)], t_out[(2 * which + 1, *at)] = split(part)


def prepare_kernel(phase_ref, amp, prop_ref, t_out, level, turned, order):
    write_tables(t_out)
    x = phase_ref[...]
    choose = chooser(x.shape[0])
    order[...] = choose
    first, rest = split(x)
    third = (x - first.astype(F32) - rest.astype(F32)).astype(BF16)
    phase = unmixed(dot(first, choose) + dot(rest, choose) + dot(third, choose), turned)
    prop_ref[0] = jnp.cos(phase)
    prop_ref[1] = jnp.sin(phase)

    @pl.loop(0, amp.shape[0])
    def _(p):
        top, low = split(amp[p])
        level[p] = unmixed(dot(top, order[...]) + dot(low, order[...]), turned)


def prepare(phase, amplitudes):
    size = phase.shape[0]
    return call(
        prepare_kernel,
        (
            shaped(2, size, size),
            jax.ShapeDtypeStruct((8, size, size), BF16),
            shaped(*amplitudes.shape),
        ),
        flops=1 << 28,
        in_specs=[VMEM, VMEM],
        out_specs=(VMEM,) * 3,
        scratch_shapes=[
            pltpu.VMEM((size // LANES, size, LANES), F32),
            pltpu.VMEM((size, size), BF16),
        ],
        name="prepare",
    )(phase, amplitudes)


def assemble(ext, tile, rows, near, far, corner_near, corner_far, odd):
    size = tile.shape[1]
    tiles = size // LANES
    spans = ((0, rows, 0, HALO), (HALO, None, 0, size), (HALO + size, rows, HALO, HALO))
    for top, strip, source, length in spans:
        here = pl.ds(top, length)
        there = pl.ds(source, length)
        for c in range(2):
            for j in range(tiles):
                across = slice(j * LANES, (j + 1) * LANES)
                ext[c, j + 1, here] = (
                    tile[c, :, across] if strip is None else strip[c, there, across]
                )
        w, h = swapped(
            odd,
            near[...] if strip is None else corner_near[there, :],
            far[...] if strip is None else corner_far[there, :],
        )
        ext[0, 0, here] = h
        ext[1, 0, here] = pltpu.roll(h, HALO, 1)
        ext[0, tiles + 1, here] = w
        ext[1, tiles + 1, here] = pltpu.roll(w, HALO, 1)


def place(off_ref, p):
    col = off_ref[1, p] + HALO
    return off_ref[0, p], col // LANES, col % LANES


def window(ext, off_ref, p, c, size):
    row, tile, turn = place(off_ref, p)
    keep = lax.broadcasted_iota(jnp.int32, (size, LANES), 1) < LANES - turn
    turned = [
        pltpu.roll(ext[c, tile + j, pl.ds(row, size), :], LANES - turn, 1)
        for j in range(size // LANES + 1)
    ]
    return jnp.concatenate(
        [jnp.where(keep, turned[j], turned[j + 1]) for j in range(size // LANES)], 1
    )


def add_window(acc, off_ref, p, c, value):
    size = value.shape[0]
    row, tile, turn = place(off_ref, p)
    keep = lax.broadcasted_iota(jnp.int32, (size, LANES), 1) >= turn
    count = size // LANES
    turned = [pltpu.roll(value[:, j * LANES : (j + 1) * LANES], turn, 1) for j in range(count)]
    zero = jnp.zeros((size, LANES), F32)
    before = [zero] + turned
    after = turned + [zero]
    for j in range(count + 1):
        at = (c, tile + j, pl.ds(row, size))
        acc[at] = acc[at] + jnp.where(keep, after[j], before[j])


def times(ar, ai, br, bi):
    return ar * br - ai * bi, ar * bi + ai * br


def conj_times(ar, ai, br, bi):
    return ar * br + ai * bi, ar * bi - ai * br


def first_kernel(off, x, rows, near, far, cn, cf, probe, prop, t, psi_out, w_out, ext, *buffers):
    stage = Stage(t, *buffers)
    count, _, size, _ = psi_out.shape
    many = len(stage.group)
    h = stage.half
    assemble(ext, x.at[0], rows, near.at[0], far.at[0], cn, cf, on_odd())

    @pl.loop(0, count // many)
    def _(i):
        first = i * many

        def source(q):
            w = [window(ext, off, first + q, c, size) for c in (0, 1)]
            w_out[first + q, 0], w_out[first + q, 1] = w
            return times(probe[0], probe[1], *w)

        def change(q, e, re, im):
            here = slice(e * h, (e + 1) * h)
            return times(prop[0, here], prop[1, here], re, im)

        def sink(q, re, im):
            psi_out[first + q, 0], psi_out[first + q, 1] = re, im

        stage.forward(source)
        stage.inverse(change, sink)


def second_kernel(
    off, x, rows, near, far, corners, psi, level, t, u_out, beta_out, ext, kept, *buffers
):
    stage = Stage(t, *buffers)
    count, _, size, _ = psi.shape
    many = len(stage.group)
    h = stage.half
    assemble(ext, x.at[1], rows, near.at[1], far.at[1], corners.at[0], corners.at[1], on_odd())

    @pl.loop(0, count // many)
    def _(i):
        first = i * many

        def source(q):
            w = [window(ext, off, first + q, c, size) for c in (0, 1)]
            kept[q, 0], kept[q, 1] = w
            return times(psi[first + q, 0], psi[first + q, 1], *w)

        def change(q, e, re, im):
            magnitude = jnp.sqrt(re * re + im * im)
            keep = 1.0 - level[first + q, e * h : (e + 1) * h] / jnp.maximum(magnitude, 0.5)
            return re * keep, im * keep

        def sink(q, re, im):
            p = first + q
            u_out[p, 0], u_out[p, 1] = conj_times(kept[q, 0], kept[q, 1], re, im)
            beta_out[p, 0], beta_out[p, 1] = re, im

        stage.forward(source)
        stage.inverse(change, sink)


def third_kernel(factor, u, w, prop, t, beta_out, mine_out, other_out, acc, *buffers):
    stage = Stage(t, *buffers)
    count = u.shape[0]
    many = len(stage.group)
    h = stage.half
    acc[...] = jnp.zeros_like(acc)

    @pl.loop(0, count // many)
    def _(i):
        first = i * many

        def source(q):
            return u[first + q, 0], u[first + q, 1]

        def change(q, e, re, im):
            here = slice(e * h, (e + 1) * h)
            return conj_times(prop[0, here], prop[1, here], re, im)

        def sink(q, re, im):
            p = first + q
            beta_out[p, 0], beta_out[p, 1] = re, im
            for c, g in enumerate(conj_times(w[p, 0], w[p, 1], re, im)):
                acc[c] += g

        stage.forward(source)
        stage.inverse(change, sink)

    mine_out[...] = acc[upper(0)] * factor
    other_out[...] = acc[1 - upper(0)] * factor


def spread_kernel(off, beta, wave, acc, near, far):
    acc[...] = jnp.zeros_like(acc)

    @pl.loop(0, beta.shape[0])
    def _(p):
        psi = wave.at[p] if len(wave.shape) == 4 else wave
        for c, g in enumerate(conj_times(psi[0], psi[1], beta[p, 0], beta[p, 1])):
            add_window(acc, off, p, c, g)

    last = acc.shape[1] - 1
    near[...], far[...] = swapped(
        on_odd(), low_rim(acc[0, last], acc[1, last]), high_rim(acc[0, 0], acc[1, 0])
    )


def rim_parts(near, far, odd, c):
    h, w = swapped(odd, near, far)
    if c:
        h, w = pltpu.roll(h, HALO, 1), pltpu.roll(w, HALO, 1)
    lane = lax.broadcasted_iota(jnp.int32, h.shape, 1)
    return jnp.where(lane < HALO, 0.0, h), jnp.where(lane < HALO, w, 0.0)


def merge_kernel(acc, near, far, strip_ref):
    tiles = acc.shape[1] - 2
    end = near.shape[0] - HALO
    for c in range(2):
        for i, start in enumerate((0, end)):
            here, there = pl.ds(i * HALO, HALO), pl.ds(start, HALO)
            h, w = rim_parts(near[there], far[there], on_odd(), c)
            for j in range(tiles):
                value = acc[c, j + 1, there]
                if j == 0:
                    value += w
                if j == tiles - 1:
                    value += h
                strip_ref[c, here, j * LANES : (j + 1) * LANES] = value


def finish_kernel(acc, near, far, strip, *refs):
    out_ref = refs[-1]
    size = out_ref.shape[2]
    tiles = size // LANES
    middle = pl.ds(HALO, size)
    for c in range(2):
        h, w = rim_parts(near[middle], far[middle], on_odd(), c)
        for j in range(tiles):
            value = acc[c, j + 1, middle]
            if j == 0:
                value += w
            if j == tiles - 1:
                value += h
            across = slice(j * LANES, (j + 1) * LANES)
            out_ref[0, c, HALO:-HALO, across] = value[HALO:-HALO]
            out_ref[0, c, :HALO, across] = value[:HALO] + strip[c, HALO:, across]
            out_ref[0, c, -HALO:, across] = value[-HALO:] + strip[c, :HALO, across]


def finish(s, shape, arrays, before=()):
    return call(
        finish_kernel,
        shaped(*shape),
        room=16,
        grid=(1,),
        in_specs=[VMEM] * 4 + [pl.BlockSpec(memory_space=pl.ANY)] * len(before),
        out_specs=pl.BlockSpec((1, *shape[1:]), lambda i: (s, 0, 0, 0)),
        input_output_aliases={4: 0} if before else {},
        name="finish",
    )(*arrays, *before)


def shift(x, axis, by):
    count = lax.axis_size(axis)
    return lax.ppermute(x, axis, [(i, (i + by) % count) for i in range(count)])


def exchange(near, far):
    count = lax.axis_size("col")
    far = lax.ppermute(far, "col", [(i, (i + i % 2 * 2 - 1) % count) for i in range(count)])
    near = lax.ppermute(near, "col", [(i, i ^ 1) for i in range(count)])
    return near, far


def to_both(strips, axis, width, by):
    if lax.axis_size(axis) == 2:
        return shift(strips, axis, 1)
    return jnp.concatenate(
        [shift(strips[:, :width], axis, by), shift(strips[:, width:], axis, -by)], axis=1
    )


def halving_kernel(at, mine, came, mine_out, other_out):
    half = mine_out.shape[0]
    here = pl.ds(pl.multiple_of(upper(at) * half, half), half)
    there = pl.ds(pl.multiple_of((1 - upper(at)) * half, half), half)
    mine_out[...] = mine[here] + came[here]
    other_out[...] = mine[there] + came[there]


def adding_kernel(mine, came, out):
    out[...] = mine[...] + came[...]


def joining_kernel(at, mine, came, out):
    half = mine.shape[0]
    out[pl.ds(pl.multiple_of(upper(at) * half, half), half)] = mine[...]
    out[pl.ds(pl.multiple_of((1 - upper(at)) * half, half), half)] = came[...]


def ending_kernel(mine, came, out, sem):
    copies = [
        pltpu.make_async_copy(mine, out.at[upper(0)], sem.at[0]),
        pltpu.make_async_copy(came, out.at[1 - upper(0)], sem.at[1]),
    ]
    for copy in copies:
        copy.start()
    for copy in copies:
        copy.wait()


def halvings():
    return [("col", bit) for bit in (1, 2, 4) if bit < lax.axis_size("col")]


def total(mine, other):
    sizes = {axis: lax.axis_size(axis) for axis in ("row", "col")}
    halves = halvings()
    rest = []
    for axis in ("row", "col"):
        bit = 1
        while bit < sizes[axis]:
            if (axis, bit) not in halves:
                rest.append((axis, bit))
            bit *= 2

    def swap(y, axis, bit):
        return lax.ppermute(y, axis, [(i, i ^ bit) for i in range(sizes[axis])])

    def add(x, came):
        return call(
            adding_kernel, shaped(*x.shape), in_specs=[VMEM] * 2, out_specs=VMEM, name="adding"
        )(x, came)

    for at, (axis, bit) in enumerate(halves):
        came = swap(other, axis, bit)
        if at + 1 == len(halves):
            x = add(mine, came)
            break
        out = shaped(mine.shape[0] // 2, mine.shape[1])
        mine, other = call(
            functools.partial(halving_kernel, at + 1),
            (out, out),
            in_specs=[VMEM, VMEM],
            out_specs=(VMEM, VMEM),
            name="halving",
        )(mine, came)
    for axis, bit in rest:
        x = add(x, swap(x, axis, bit))
    for at, (axis, bit) in reversed(list(enumerate(halves))):
        came = swap(x, axis, bit)
        if at == 0:
            return call(
                ending_kernel,
                shaped(2, *x.shape),
                in_specs=[VMEM, VMEM],
                out_specs=pl.BlockSpec(memory_space=pltpu.HBM),
                scratch_shapes=[pltpu.SemaphoreType.DMA((2,))],
                name="ending",
            )(x, came)
        x = call(
            functools.partial(joining_kernel, at),
            shaped(2 * x.shape[0], x.shape[1]),
            in_specs=[VMEM, VMEM],
            out_specs=VMEM,
            name="joining",
        )(x, came)


def local(object_field, offsets, amplitudes, probe, phase):
    tile = object_field.shape[2]
    size = probe.shape[1]
    count = offsets.shape[0]
    off = jnp.transpose(offsets[:, 0])
    span = tile + 2 * HALO
    ext = pltpu.VMEM((2, tile // LANES + 2, span, LANES), F32)
    flops = count * 2 * 4 * 3 * 2 * size**3

    edges0 = cut_rows(object_field, 0)
    near, far = cut(object_field)
    edges1 = cut_rows(object_field, 1)
    rows0 = to_both(edges0, "row", HALO, 1)
    near, far = exchange(near, far)
    prop, t, level = prepare(phase, amplitudes[:, 0])
    rows1 = to_both(edges1, "row", HALO, 1)
    corner_near, corner_far = row_corners(rows0)
    corner_near, corner_far = exchange(corner_near, corner_far)
    corners1 = rim_corners(near, far, 1)
    corners1 = to_both(corners1, "row", HALO, 1)

    field = shaped(count, 2, size, size)
    buffers = stage_scratch(count, size)
    many = group_of(count)
    everyone = count * lax.axis_size("row") * lax.axis_size("col")
    factor = 1.0 / math.sqrt(everyone)
    psi, w0 = call(
        first_kernel,
        (field, field),
        flops=flops,
        room=ROOM,
        in_specs=[SMEM] + [VMEM] * 9,
        out_specs=(VMEM,) * 2,
        scratch_shapes=[ext, *buffers],
        name="first",
    )(off, object_field, rows0, near, far, corner_near, corner_far, probe, prop, t)
    u, beta1 = call(
        second_kernel,
        (field, field),
        flops=flops,
        room=ROOM,
        in_specs=[SMEM] + [VMEM] * 8,
        out_specs=(VMEM,) * 2,
        scratch_shapes=[ext, pltpu.VMEM((many, 2, size, size), F32), *buffers],
        name="second",
    )(off, object_field, rows1, near, far, corners1, psi, level, t)
    beta, mine, other = call(
        functools.partial(third_kernel, factor),
        (field, shaped(size, size), shaped(size, size)),
        flops=flops,
        room=ROOM,
        in_specs=[VMEM] * 4,
        out_specs=(VMEM,) * 3,
        scratch_shapes=[pltpu.VMEM((2, size, size), F32), *buffers],
        name="third",
    )(u, w0, prop, t)

    def spread(beta, wave):
        return call(
            spread_kernel,
            (shaped(*ext.shape), shaped(span, LANES), shaped(span, LANES)),
            room=ROOM,
            in_specs=[SMEM] + [VMEM] * 2,
            out_specs=(VMEM,) * 3,
            name="spread",
        )(off, beta, wave)

    sum1, near1, far1 = spread(beta1, psi)
    near1, far1 = exchange(near1, far1)
    sum0, near0, far0 = spread(beta, probe)
    near0, far0 = exchange(near0, far0)
    merge = call(
        merge_kernel,
        shaped(2, 2 * HALO, tile),
        in_specs=[VMEM] * 3,
        out_specs=VMEM,
        name="merge",
    )
    strip1 = merge(sum1, near1, far1)
    back1 = to_both(strip1, "row", HALO, -1)
    strip0 = merge(sum0, near0, far0)
    back0 = to_both(strip0, "row", HALO, -1)
    grad = finish(1, object_field.shape, (sum1, near1, far1, back1))
    grad = finish(0, object_field.shape, (sum0, near0, far0, back0), (grad,))
    return grad, total(mine, other)


def solution(mesh):
    in_specs = (
        P(None, None, "row", "col"),
        P("row", "col", None),
        P("row", "col", None, None),
        P(),
        P(),
    )
    out_specs = (P(None, None, "row", "col"), P())

    return jax.shard_map(local, mesh=mesh, in_specs=in_specs, out_specs=out_specs, check_vma=False)
```

```python
import functools
import math

import jax
import jax.numpy as jnp
from jax import lax
from jax.experimental import pallas as pl
from jax.experimental.pallas import tpu as pltpu
from jax.sharding import PartitionSpec as P

HALO = 64
ROOM = 20
LANES = 128
F32 = jnp.float32
BF16 = jnp.bfloat16
VMEM = pl.BlockSpec(memory_space=pltpu.VMEM)
SMEM = pl.BlockSpec(memory_space=pltpu.SMEM)


def split(x):
    high = x.astype(BF16)
    return high, (x - high.astype(F32)).astype(BF16)


def dot(a, b):
    return jnp.dot(a, b, preferred_element_type=F32)


class Stage:
    def __init__(self, t, high, low, product):
        self.t, self.high, self.low, self.product = t, high, low, product
        self.group = range(high.shape[0])
        self.half = high.shape[2] // 2

    def put(self, q, e, x):
        self.high[q, e], self.low[q, e] = split(x)

    def right(self, q, e, which):
        th, tl = self.t[2 * which], self.t[2 * which + 1]
        high, low = self.high[q, e], self.low[q, e]
        return dot(high, th) + dot(low, th) + dot(high, tl)

    def left(self, q, e, which):
        th, tl = self.t[2 * which], self.t[2 * which + 1]
        high, low = self.high[q, e], self.low[q, e]
        return dot(th, high) + dot(th, low) + dot(tl, high)

    def forward(self, source):
        h = self.half
        for q in self.group:
            x = source(q)
            self.put(q, 0, jnp.concatenate([y[:, :h] + y[:, h:] for y in x], 1))
            self.put(q, 1, jnp.concatenate([y[:, :h] - y[:, h:] for y in x], 1))
        for q in self.group:
            self.product[q, 0] = self.right(q, 0, 0)
            self.product[q, 1] = self.right(q, 1, 2)
        for q in self.group:
            top = self.product[q, :, :h, :]
            bottom = self.product[q, :, h:, :]
            for e, y in enumerate((top + bottom, top - bottom)):
                parts = [
                    jnp.concatenate([y[k, :, c * h : (c + 1) * h] for k in (0, 1)], 1) for c in (0, 1)
                ]
                self.put(q, e, jnp.concatenate(parts, 0))
        for q in self.group:
            self.product[q, 0] = self.left(q, 0, 1)
            self.product[q, 1] = self.left(q, 1, 3)

    def inverse(self, change, sink):
        h = self.half
        for q in self.group:
            for e in (0, 1):
                z = change(q, e, self.product[q, e, :h], self.product[q, e, h:])
                self.put(q, e, jnp.concatenate(z, 0))
        for q in self.group:
            self.product[q, 0] = self.left(q, 0, 0)
            self.product[q, 1] = self.left(q, 1, 2)
        for q in self.group:
            even, odd = self.product[q, 0], self.product[q, 1]
            p, m = even + odd, even - odd
            parts = [jnp.concatenate([p[c * h : (c + 1) * h], m[c * h : (c + 1) * h]], 0) for c in (0, 1)]
            self.put(q, 0, jnp.concatenate([y[:, :h] for y in parts], 1))
            self.put(q, 1, jnp.concatenate([y[:, h:] for y in parts], 1))
        for q in self.group:
            even, odd = self.right(q, 0, 1), self.right(q, 1, 3)
            p, m = even + odd, even - odd
            sink(q, *[jnp.concatenate([y[:, c * h : (c + 1) * h] for y in (p, m)], 1) for c in (0, 1)])


def group_of(count):
    return 2 if count % 2 == 0 else 1


def stage_scratch(count, size):
    shape = (group_of(count), 2, size, size)
    return [pltpu.VMEM(shape, BF16), pltpu.VMEM(shape, BF16), pltpu.VMEM(shape, F32)]


def call(kernel, out_shape, flops=0, room=8, **kwargs):
    return pl.pallas_call(
        kernel,
        out_shape=out_shape,
        cost_estimate=pl.CostEstimate(flops=flops, bytes_accessed=4 << 20, transcendentals=0),
        compiler_params=pltpu.CompilerParams(vmem_limit_bytes=room << 20),
        **kwargs,
    )


def shaped(*shape):
    return jax.ShapeDtypeStruct(shape, F32)


def side_by_side(re, im):
    lane = lax.broadcasted_iota(jnp.int32, re.shape, 1)
    turned = pltpu.roll(im, HALO, 1)
    return lane < HALO, turned


def high_rim(re, im):
    low, turned = side_by_side(re, im)
    return jnp.where(low, turned, re)


def low_rim(re, im):
    low, turned = side_by_side(re, im)
    return jnp.where(low, re, turned)


def upper(at):
    axis, bit = halvings()[at]
    return lax.axis_index(axis) // bit % 2


def on_odd():
    return lax.axis_index("col") % 2 == 1


def swapped(odd, a, b):
    return jnp.where(odd, b, a), jnp.where(odd, a, b)


def cut_rows_kernel(s, x_ref, out):
    size = x_ref.shape[2]
    for c in range(2):
        out[c, :HALO] = x_ref[s, c, size - HALO :]
        out[c, HALO:] = x_ref[s, c, :HALO]


def cut_rows(x, s):
    return call(
        functools.partial(cut_rows_kernel, s),
        shaped(2, 2 * HALO, x.shape[2]),
        in_specs=[VMEM],
        out_specs=VMEM,
        name="cut",
    )(x)


def cut_kernel(x_ref, near, far):
    for s in range(x_ref.shape[0]):
        near[s], far[s] = swapped(
            on_odd(),
            high_rim(x_ref[s, 0, :, -LANES:], x_ref[s, 1, :, -LANES:]),
            low_rim(x_ref[s, 0, :, :LANES], x_ref[s, 1, :, :LANES]),
        )


def cut(x):
    slices, _, size, _ = x.shape
    rim = shaped(slices, size, LANES)
    return call(
        cut_kernel, (rim, rim), in_specs=[VMEM], out_specs=(VMEM,) * 2, name="cut"
    )(x)


def row_corners_kernel(rows_ref, near, far):
    near[...], far[...] = swapped(
        on_odd(),
        high_rim(rows_ref[0, :, -LANES:], rows_ref[1, :, -LANES:]),
        low_rim(rows_ref[0, :, :LANES], rows_ref[1, :, :LANES]),
    )


def row_corners(rows):
    out = shaped(2 * HALO, LANES)
    return call(
        row_corners_kernel,
        (out, out),
        in_specs=[VMEM],
        out_specs=(VMEM, VMEM),
        name="corners",
    )(rows)


def rim_corners_kernel(s, near, far, out_ref):
    for i, ref in enumerate((near, far)):
        out_ref[i, 0:HALO] = ref[s, -HALO:]
        out_ref[i, HALO:] = ref[s, 0:HALO]


def rim_corners(near, far, s):
    return call(
        functools.partial(rim_corners_kernel, s),
        shaped(2, 2 * HALO, LANES),
        in_specs=[VMEM, VMEM],
        out_specs=VMEM,
        name="corners",
    )(near, far)


def chooser(size):
    half = size // 2
    i = lax.broadcasted_iota(jnp.int32, (size, size), 0)
    j = lax.broadcasted_iota(jnp.int32, (size, size), 1)
    picked = jnp.where(j < half, 2 * j, 2 * (j - half) + 1)
    return jnp.where(i == picked, 1.0, 0.0).astype(BF16)


def unmixed(across, turned):
    size = across.shape[1]
    for k in range(size // LANES):
        turned[k] = across[:, k * LANES : (k + 1) * LANES]
    rows = []
    for odd in (0, 1):
        here = pl.ds(odd, across.shape[0] // 2, stride=2)
        rows.append(jnp.concatenate([turned[k, here, :] for k in range(size // LANES)], 1))
    return jnp.concatenate(rows, 0)


def write_tables(t_out):
    size = t_out.shape[1]
    half = size // 2
    i = lax.broadcasted_iota(jnp.int32, (half, half), 0)
    j = lax.broadcasted_iota(jnp.int32, (half, half), 1)
    products = (2 * i * j, 2 * j * i, i * (2 * j + 1), j * (2 * i + 1))
    for which, product in enumerate(products):
        angle = (product % size).astype(F32) * (2.0 * math.pi / size)
        re = jnp.cos(angle) * (1.0 / math.sqrt(size))
        im = jnp.sin(angle) * (-1.0 / math.sqrt(size))
        if which % 2:
            im = -im
        for r, row in enumerate(((re, im), (-im, re))):
            for c, part in enumerate(row):
                at = (slice(r * half, (r + 1) * half), slice(c * half, (c + 1) * half))
                t_out[(2 * which, *at)], t_out[(2 * which + 1, *at)] = split(part)


def prepare_kernel(phase_ref, amp, prop_ref, t_out, level, turned, order):
    write_tables(t_out)
    x = phase_ref[...]
    choose = chooser(x.shape[0])
    order[...] = choose
    first, rest = split(x)
    third = (x - first.astype(F32) - rest.astype(F32)).astype(BF16)
    phase = unmixed(dot(first, choose) + dot(rest, choose) + dot(third, choose), turned)
    prop_ref[0] = jnp.cos(phase)
    prop_ref[1] = jnp.sin(phase)

    @pl.loop(0, amp.shape[0])
    def _(p):
        top, low = split(amp[p])
        level[p] = unmixed(dot(top, order[...]) + dot(low, order[...]), turned)


def prepare(phase, amplitudes):
    size = phase.shape[0]
    return call(
        prepare_kernel,
        (
            shaped(2, size, size),
            jax.ShapeDtypeStruct((8, size, size), BF16),
            shaped(*amplitudes.shape),
        ),
        flops=1 << 28,
        in_specs=[VMEM, VMEM],
        out_specs=(VMEM,) * 3,
        scratch_shapes=[
            pltpu.VMEM((size // LANES, size, LANES), F32),
            pltpu.VMEM((size, size), BF16),
        ],
        name="prepare",
    )(phase, amplitudes)


def assemble(ext, tile, rows, near, far, corner_near, corner_far, odd):
    size = tile.shape[1]
    tiles = size // LANES
    spans = ((0, rows, 0, HALO), (HALO, None, 0, size), (HALO + size, rows, HALO, HALO))
    for top, strip, source, length in spans:
        here = pl.ds(top, length)
        there = pl.ds(source, length)
        for c in range(2):
            for j in range(tiles):
                across = slice(j * LANES, (j + 1) * LANES)
                ext[c, j + 1, here] = (
                    tile[c, :, across] if strip is None else strip[c, there, across]
                )
        w, h = swapped(
            odd,
            near[...] if strip is None else corner_near[there, :],
            far[...] if strip is None else corner_far[there, :],
        )
        ext[0, 0, here] = h
        ext[1, 0, here] = pltpu.roll(h, HALO, 1)
        ext[0, tiles + 1, here] = w
        ext[1, tiles + 1, here] = pltpu.roll(w, HALO, 1)


def place(off_ref, p):
    col = off_ref[1, p] + HALO
    return off_ref[0, p], col // LANES, col % LANES


def window(ext, off_ref, p, c, size):
    row, tile, turn = place(off_ref, p)
    keep = lax.broadcasted_iota(jnp.int32, (size, LANES), 1) < LANES - turn
    turned = [
        pltpu.roll(ext[c, tile + j, pl.ds(row, size), :], LANES - turn, 1)
        for j in range(size // LANES + 1)
    ]
    return jnp.concatenate(
        [jnp.where(keep, turned[j], turned[j + 1]) for j in range(size // LANES)], 1
    )


def add_window(acc, off_ref, p, c, value):
    size = value.shape[0]
    row, tile, turn = place(off_ref, p)
    keep = lax.broadcasted_iota(jnp.int32, (size, LANES), 1) >= turn
    count = size // LANES
    turned = [pltpu.roll(value[:, j * LANES : (j + 1) * LANES], turn, 1) for j in range(count)]
    zero = jnp.zeros((size, LANES), F32)
    before = [zero] + turned
    after = turned + [zero]
    for j in range(count + 1):
        at = (c, tile + j, pl.ds(row, size))
        acc[at] = acc[at] + jnp.where(keep, after[j], before[j])


def times(ar, ai, br, bi):
    return ar * br - ai * bi, ar * bi + ai * br


def conj_times(ar, ai, br, bi):
    return ar * br + ai * bi, ar * bi - ai * br


def first_kernel(off, x, rows, near, far, cn, cf, probe, prop, t, psi_out, w_out, ext, *buffers):
    stage = Stage(t, *buffers)
    count, _, size, _ = psi_out.shape
    many = len(stage.group)
    h = stage.half
    assemble(ext, x.at[0], rows, near.at[0], far.at[0], cn, cf, on_odd())

    @pl.loop(0, count // many, unroll=True)
    def _(i):
        first = i * many

        def source(q):
            w = [window(ext, off, first + q, c, size) for c in (0, 1)]
            w_out[first + q, 0], w_out[first + q, 1] = w
            return times(probe[0], probe[1], *w)

        def change(q, e, re, im):
            here = slice(e * h, (e + 1) * h)
            return times(prop[0, here], prop[1, here], re, im)

        def sink(q, re, im):
            psi_out[first + q, 0], psi_out[first + q, 1] = re, im

        stage.forward(source)
        stage.inverse(change, sink)


def second_kernel(
    off, x, rows, near, far, corners, psi, level, t, u_out, beta_out, ext, kept, *buffers
):
    stage = Stage(t, *buffers)
    count, _, size, _ = psi.shape
    many = len(stage.group)
    h = stage.half
    assemble(ext, x.at[1], rows, near.at[1], far.at[1], corners.at[0], corners.at[1], on_odd())

    @pl.loop(0, count // many, unroll=True)
    def _(i):
        first = i * many

        def source(q):
            w = [window(ext, off, first + q, c, size) for c in (0, 1)]
            kept[q, 0], kept[q, 1] = w
            return times(psi[first + q, 0], psi[first + q, 1], *w)

        def change(q, e, re, im):
            magnitude = jnp.sqrt(re * re + im * im)
            keep = 1.0 - level[first + q, e * h : (e + 1) * h] / jnp.maximum(magnitude, 0.5)
            return re * keep, im * keep

        def sink(q, re, im):
            p = first + q
            u_out[p, 0], u_out[p, 1] = conj_times(kept[q, 0], kept[q, 1], re, im)
            beta_out[p, 0], beta_out[p, 1] = re, im

        stage.forward(source)
        stage.inverse(change, sink)


def third_kernel(factor, u, w, prop, t, beta_out, mine_out, other_out, acc, *buffers):
    stage = Stage(t, *buffers)
    count = u.shape[0]
    many = len(stage.group)
    h = stage.half
    acc[...] = jnp.zeros_like(acc)

    @pl.loop(0, count // many, unroll=True)
    def _(i):
        first = i * many

        def source(q):
            return u[first + q, 0], u[first + q, 1]

        def change(q, e, re, im):
            here = slice(e * h, (e + 1) * h)
            return conj_times(prop[0, here], prop[1, here], re, im)

        def sink(q, re, im):
            p = first + q
            beta_out[p, 0], beta_out[p, 1] = re, im
            for c, g in enumerate(conj_times(w[p, 0], w[p, 1], re, im)):
                acc[c] += g

        stage.forward(source)
        stage.inverse(change, sink)

    mine_out[...] = acc[upper(0)] * factor
    other_out[...] = acc[1 - upper(0)] * factor


def spread_kernel(off, beta, wave, acc, near, far):
    acc[...] = jnp.zeros_like(acc)

    @pl.loop(0, beta.shape[0], unroll=True)
    def _(p):
        psi = wave.at[p] if len(wave.shape) == 4 else wave
        for c, g in enumerate(conj_times(psi[0], psi[1], beta[p, 0], beta[p, 1])):
            add_window(acc, off, p, c, g)

    last = acc.shape[1] - 1
    near[...], far[...] = swapped(
        on_odd(), low_rim(acc[0, last], acc[1, last]), high_rim(acc[0, 0], acc[1, 0])
    )


def rim_parts(near, far, odd, c):
    h, w = swapped(odd, near, far)
    if c:
        h, w = pltpu.roll(h, HALO, 1), pltpu.roll(w, HALO, 1)
    lane = lax.broadcasted_iota(jnp.int32, h.shape, 1)
    return jnp.where(lane < HALO, 0.0, h), jnp.where(lane < HALO, w, 0.0)


def merge_kernel(acc, near, far, strip_ref):
    tiles = acc.shape[1] - 2
    end = near.shape[0] - HALO
    for c in range(2):
        for i, start in enumerate((0, end)):
            here, there = pl.ds(i * HALO, HALO), pl.ds(start, HALO)
            h, w = rim_parts(near[there], far[there], on_odd(), c)
            for j in range(tiles):
                value = acc[c, j + 1, there]
                if j == 0:
                    value += w
                if j == tiles - 1:
                    value += h
                strip_ref[c, here, j * LANES : (j + 1) * LANES] = value


def finish_kernel(acc, near, far, strip, *refs):
    out_ref = refs[-1]
    size = out_ref.shape[2]
    tiles = size // LANES
    middle = pl.ds(HALO, size)
    for c in range(2):
        h, w = rim_parts(near[middle], far[middle], on_odd(), c)
        for j in range(tiles):
            value = acc[c, j + 1, middle]
            if j == 0:
                value += w
            if j == tiles - 1:
                value += h
            across = slice(j * LANES, (j + 1) * LANES)
            out_ref[0, c, HALO:-HALO, across] = value[HALO:-HALO]
            out_ref[0, c, :HALO, across] = value[:HALO] + strip[c, HALO:, across]
            out_ref[0, c, -HALO:, across] = value[-HALO:] + strip[c, :HALO, across]


def finish(s, shape, arrays, before=()):
    return call(
        finish_kernel,
        shaped(*shape),
        room=16,
        grid=(1,),
        in_specs=[VMEM] * 4 + [pl.BlockSpec(memory_space=pl.ANY)] * len(before),
        out_specs=pl.BlockSpec((1, *shape[1:]), lambda i: (s, 0, 0, 0)),
        input_output_aliases={4: 0} if before else {},
        name="finish",
    )(*arrays, *before)


def shift(x, axis, by):
    count = lax.axis_size(axis)
    return lax.ppermute(x, axis, [(i, (i + by) % count) for i in range(count)])


def exchange(near, far):
    count = lax.axis_size("col")
    far = lax.ppermute(far, "col", [(i, (i + i % 2 * 2 - 1) % count) for i in range(count)])
    near = lax.ppermute(near, "col", [(i, i ^ 1) for i in range(count)])
    return near, far


def to_both(strips, axis, width, by):
    if lax.axis_size(axis) == 2:
        return shift(strips, axis, 1)
    return jnp.concatenate(
        [shift(strips[:, :width], axis, by), shift(strips[:, width:], axis, -by)], axis=1
    )


def halving_kernel(at, mine, came, mine_out, other_out):
    half = mine_out.shape[0]
    here = pl.ds(pl.multiple_of(upper(at) * half, half), half)
    there = pl.ds(pl.multiple_of((1 - upper(at)) * half, half), half)
    mine_out[...] = mine[here] + came[here]
    other_out[...] = mine[there] + came[there]


def adding_kernel(mine, came, out):
    out[...] = mine[...] + came[...]


def joining_kernel(at, mine, came, out):
    half = mine.shape[0]
    out[pl.ds(pl.multiple_of(upper(at) * half, half), half)] = mine[...]
    out[pl.ds(pl.multiple_of((1 - upper(at)) * half, half), half)] = came[...]


def ending_kernel(mine, came, out, sem):
    copies = [
        pltpu.make_async_copy(mine, out.at[upper(0)], sem.at[0]),
        pltpu.make_async_copy(came, out.at[1 - upper(0)], sem.at[1]),
    ]
    for copy in copies:
        copy.start()
    for copy in copies:
        copy.wait()


def halvings():
    return [("col", bit) for bit in (1, 2, 4) if bit < lax.axis_size("col")]


def total(mine, other):
    sizes = {axis: lax.axis_size(axis) for axis in ("row", "col")}
    halves = halvings()
    rest = []
    for axis in ("row", "col"):
        bit = 1
        while bit < sizes[axis]:
            if (axis, bit) not in halves:
                rest.append((axis, bit))
            bit *= 2

    def swap(y, axis, bit):
        return lax.ppermute(y, axis, [(i, i ^ bit) for i in range(sizes[axis])])

    def add(x, came):
        return call(
            adding_kernel, shaped(*x.shape), in_specs=[VMEM] * 2, out_specs=VMEM, name="adding"
        )(x, came)

    for at, (axis, bit) in enumerate(halves):
        came = swap(other, axis, bit)
        if at + 1 == len(halves):
            x = add(mine, came)
            break
        out = shaped(mine.shape[0] // 2, mine.shape[1])
        mine, other = call(
            functools.partial(halving_kernel, at + 1),
            (out, out),
            in_specs=[VMEM, VMEM],
            out_specs=(VMEM, VMEM),
            name="halving",
        )(mine, came)
    for axis, bit in rest:
        x = add(x, swap(x, axis, bit))
    for at, (axis, bit) in reversed(list(enumerate(halves))):
        came = swap(x, axis, bit)
        if at == 0:
            return call(
                ending_kernel,
                shaped(2, *x.shape),
                in_specs=[VMEM, VMEM],
                out_specs=pl.BlockSpec(memory_space=pltpu.HBM),
                scratch_shapes=[pltpu.SemaphoreType.DMA((2,))],
                name="ending",
            )(x, came)
        x = call(
            functools.partial(joining_kernel, at),
            shaped(2 * x.shape[0], x.shape[1]),
            in_specs=[VMEM, VMEM],
            out_specs=VMEM,
            name="joining",
        )(x, came)


def local(object_field, offsets, amplitudes, probe, phase):
    tile = object_field.shape[2]
    size = probe.shape[1]
    count = offsets.shape[0]
    off = jnp.transpose(offsets[:, 0])
    span = tile + 2 * HALO
    ext = pltpu.VMEM((2, tile // LANES + 2, span, LANES), F32)
    flops = count * 2 * 4 * 3 * 2 * size**3

    edges0 = cut_rows(object_field, 0)
    near, far = cut(object_field)
    edges1 = cut_rows(object_field, 1)
    rows0 = to_both(edges0, "row", HALO, 1)
    near, far = exchange(near, far)
    prop, t, level = prepare(phase, amplitudes[:, 0])
    rows1 = to_both(edges1, "row", HALO, 1)
    corner_near, corner_far = row_corners(rows0)
    corner_near, corner_far = exchange(corner_near, corner_far)
    corners1 = rim_corners(near, far, 1)
    corners1 = to_both(corners1, "row", HALO, 1)

    field = shaped(count, 2, size, size)
    buffers = stage_scratch(count, size)
    many = group_of(count)
    everyone = count * lax.axis_size("row") * lax.axis_size("col")
    factor = 1.0 / math.sqrt(everyone)
    psi, w0 = call(
        first_kernel,
        (field, field),
        flops=flops,
        room=ROOM,
        in_specs=[SMEM] + [VMEM] * 9,
        out_specs=(VMEM,) * 2,
        scratch_shapes=[ext, *buffers],
        name="first",
    )(off, object_field, rows0, near, far, corner_near, corner_far, probe, prop, t)
    u, beta1 = call(
        second_kernel,
        (field, field),
        flops=flops,
        room=ROOM,
        in_specs=[SMEM] + [VMEM] * 8,
        out_specs=(VMEM,) * 2,
        scratch_shapes=[ext, pltpu.VMEM((many, 2, size, size), F32), *buffers],
        name="second",
    )(off, object_field, rows1, near, far, corners1, psi, level, t)
    beta, mine, other = call(
        functools.partial(third_kernel, factor),
        (field, shaped(size, size), shaped(size, size)),
        flops=flops,
        room=ROOM,
        in_specs=[VMEM] * 4,
        out_specs=(VMEM,) * 3,
        scratch_shapes=[pltpu.VMEM((2, size, size), F32), *buffers],
        name="third",
    )(u, w0, prop, t)

    def spread(beta, wave):
        return call(
            spread_kernel,
            (shaped(*ext.shape), shaped(span, LANES), shaped(span, LANES)),
            room=ROOM,
            in_specs=[SMEM] + [VMEM] * 2,
            out_specs=(VMEM,) * 3,
            name="spread",
        )(off, beta, wave)

    sum1, near1, far1 = spread(beta1, psi)
    near1, far1 = exchange(near1, far1)
    sum0, near0, far0 = spread(beta, probe)
    near0, far0 = exchange(near0, far0)
    merge = call(
        merge_kernel,
        shaped(2, 2 * HALO, tile),
        in_specs=[VMEM] * 3,
        out_specs=VMEM,
        name="merge",
    )
    strip1 = merge(sum1, near1, far1)
    back1 = to_both(strip1, "row", HALO, -1)
    strip0 = merge(sum0, near0, far0)
    back0 = to_both(strip0, "row", HALO, -1)
    grad = finish(1, object_field.shape, (sum1, near1, far1, back1))
    grad = finish(0, object_field.shape, (sum0, near0, far0, back0), (grad,))
    return grad, total(mine, other)


def solution(mesh):
    in_specs = (
        P(None, None, "row", "col"),
        P("row", "col", None),
        P("row", "col", None, None),
        P(),
        P(),
    )
    out_specs = (P(None, None, "row", "col"), P())

    return jax.shard_map(local, mesh=mesh, in_specs=in_specs, out_specs=out_specs, check_vma=False)
```
